32 devices in a mesh: cases: 2 (over x), box: 16 (over z, y, core).
Axes of the slice: x: 2, y: 2, z: 4, core: 2. Of those that a mesh axis runs over, the one named last changes fastest.
Arguments:
- positions: float32 [2048, 3, 128], P(('cases', 'box')), parts along dimension 0, may hold values from -9 to 9, as said below
- strengths: float32 [2048, 3, 128], P(('cases', 'box')), parts along dimension 0, may hold values from -12 to 12
- history: float32 [2048, 2, 3, 128], P(('cases', 'box')), parts along dimension 0, may hold values from -5 to 5
- move_list: int32 [2048], P(('cases', 'box')), parts along dimension 0, may hold values from 0 to 1023, as said below
- age_slot: int32 [2048], P(('cases', 'box')), parts along dimension 0, may hold values from 0 to 1023, as said below
- fetch_list: int32 [32, 16, 8], P(('cases', 'box')), parts along dimension 0, may hold values from -1 to 63, as said below
- tile_slot: int32 [2048, 32], P(('cases', 'box')), parts along dimension 0, may hold values from 0 to 127, as said below
- tile_count: int32 [2048], P(('cases', 'box')), parts along dimension 0, may hold values from 1 to 32, as said below
- blade_id: int32 [2048, 128], P(('cases', 'box')), parts along dimension 0, may hold values from 0 to 17
- hub_centre: float32 [12, 3], P('cases'), parts along dimension 0, may hold values from -8 to 8
- azimuth: float32 [12], P('cases'), parts along dimension 0, may hold values from -3.140625 to 3.140625
Outputs:
- new_positions: float32 [2048, 3, 128], P(('cases', 'box')), parts along dimension 0
- new_history: float32 [2048, 2, 3, 128], P(('cases', 'box')), parts along dimension 0
- frame: float32 [2048, 3, 128], P(('cases', 'box')), parts along dimension 0
The draws below stay inside these ranges and needn't reach their ends.
There are 2 independent parts, one for each index of `cases`. The reference program is written for one: setup_inputs(seed, part) draws one part's arguments, and reference() takes and returns one part's arrays. A program takes and returns all parts, laid end to end along the dimension named above; each array names one. Nothing has to cross between parts.
Inputs may be any that keep to these rules, and one draw needn't show every extreme that they name: Node positions; the first component of a block's nodes is offset by an amount that grows with the block's device. `move_list`: A permutation of block ids (block id = device * 64 + local block). Each device receives 64 blocks; the blocks of one device go at most 8 to any one device, and every device sends exactly 8 to some device. `age_slot`: A permutation of block ids, with the same bounds per pair of devices as move_list. `fetch_list`: entry [r, o, i] is -1 or a local block of device o; live entries come first in each [r, o] row and are distinct; rows [r, o] with o within two of r around the axis have 8 live entries. `tile_slot`: every entry names a live entry of fetch_list for the target block's device; tiles may repeat. `tile_count`: the first block of each device has 32.
All inputs are finite; a program needn't handle non-finite values.
Results may differ from the reference program's by a relative error of at most 0.0003.
Values sent between devices are 32-bit elements; how exact they have to be, the bound alone decides.
No kernel may reach another device: no remote copies, remote signals or barrier semaphores. Data moves between devices by JAX's collectives and lax.ppermute only.
A program may use at most 128 MiB of HBM per device.

```python
import math
import jax
import jax.numpy as jnp
from jax import lax

BLK = 128
NB_DEV = 64
KMAX = 32
RCAP = 8
ROTORS = 6
BLADES = 3
NBLK = 1024
N_BOX = 16


def draw_positions(key, part):
    inner = jax.random.fold_in(key, 31)
    noise = jnp.clip(jax.random.normal(inner, (NBLK, 3, BLK), jnp.float32), -5.9, 5.9)
    device = (jnp.arange(NBLK, dtype=jnp.int32) // NB_DEV).astype(jnp.float32)
    offset = 6.0 * device / N_BOX - 3.0
    shift = jnp.stack([offset, jnp.zeros_like(offset), jnp.zeros_like(offset)], axis=1)[:, :, None]
    return noise + shift


def relabel_blocks(key):
    box_count = N_BOX
    per_box = NB_DEV
    half = per_box // box_count
    quarter = box_count // 4
    key_order, key_label, key_rows, key_slots = jax.random.split(key, 4)
    position = jax.random.permutation(key_order, box_count)
    counts = half + jnp.where(position < quarter, half, 0) - jnp.where((position >= quarter) & (position < 2 * quarter), half, 0)
    offsets = jnp.repeat(jnp.arange(box_count, dtype=jnp.int32), counts, total_repeat_length=per_box)
    relabel = jax.random.permutation(key_label, box_count)
    dest = relabel[(jnp.arange(box_count, dtype=jnp.int32)[:, None] + offsets[None, :]) % box_count]
    row_perm = jax.vmap(lambda inner: jax.random.permutation(inner, per_box))(jax.random.split(key_rows, box_count))
    dest = jnp.take_along_axis(dest, row_perm, axis=1)
    flat = dest.reshape(-1)
    total = box_count * per_box
    sorted_at = jnp.argsort(flat, stable=True)
    ranking = jnp.zeros((total,), jnp.int32).at[sorted_at].set(jnp.arange(total, dtype=jnp.int32) - flat[sorted_at] * per_box)
    slot_perm = jax.vmap(lambda inner: jax.random.permutation(inner, per_box))(jax.random.split(key_slots, box_count))
    local = slot_perm[flat, ranking]
    return (flat * per_box + local).astype(jnp.int32)


def draw_move_list(key, part):
    return relabel_blocks(jax.random.fold_in(key, 11))


def draw_age_slot(key, part):
    return relabel_blocks(jax.random.fold_in(key, 23))


def fetch_tables(key):
    base = jax.random.fold_in(key, 5)
    key_live, key_ids, key_near, key_far, key_coin, key_pick, key_count = jax.random.split(base, 7)
    rows = jnp.arange(N_BOX, dtype=jnp.int32)
    gap = jnp.abs(rows[:, None] - rows[None, :])
    gap = jnp.minimum(gap, N_BOX - gap)
    far_live = jax.random.randint(key_live, (N_BOX, N_BOX), 0, 3)
    live = jnp.where(gap <= 2, RCAP, far_live)
    picks = jax.vmap(lambda inner: jax.random.permutation(inner, NB_DEV)[:RCAP])(jax.random.split(key_ids, N_BOX * N_BOX))
    picks = picks.reshape(N_BOX, N_BOX, RCAP)
    fetch = jnp.where(jnp.arange(RCAP)[None, None, :] < live[:, :, None], picks, -1).astype(jnp.int32)
    block_ids = jnp.arange(NBLK, dtype=jnp.int32)
    device = block_ids // NB_DEV
    near_owner = (device[:, None] + jax.random.randint(key_near, (NBLK, KMAX), -2, 3)) % N_BOX
    far_owner = jax.random.randint(key_far, (NBLK, KMAX), 0, N_BOX)
    use_far = (jax.random.randint(key_coin, (NBLK, KMAX), 0, 4) == 0) & (live[device[:, None], far_owner] > 0)
    owner = jnp.where(use_far, far_owner, near_owner)
    owner = owner.at[:, 0].set(device)
    chosen_live = jnp.maximum(live[device[:, None], owner], 1)
    within = jax.random.randint(key_pick, (NBLK, KMAX), 0, 1 << 20) % chosen_live
    within = within.at[:, 0].set(0)
    slot = (owner * RCAP + within).astype(jnp.int32)
    count = jax.random.randint(key_count, (NBLK,), 1, KMAX + 1)
    count = jnp.where(block_ids % NB_DEV == 0, KMAX, count).astype(jnp.int32)
    return (fetch, slot, count)


def draw_fetch_list(key, part):
    return fetch_tables(key)[0]


def draw_tile_slot(key, part):
    return fetch_tables(key)[1]


def draw_tile_count(key, part):
    return fetch_tables(key)[2]


def plant(values, rng, low, largest):
    longest = values.shape.index(max(values.shape))
    spots = []
    for shift in (0, 1):
        where = [jax.random.randint(jax.random.fold_in(rng, axis), (), 0, length) for axis, length in enumerate(values.shape)]
        where[longest] = (where[longest] + shift) % values.shape[longest]
        spots.append(tuple(where))
    return values.at[spots[0]].set(low).at[spots[1]].set(largest)


def block_levels(key, shape, pieces, least, largest):
    gain = 1.0
    for dim, shards_of in pieces:
        steps = jax.random.uniform(jax.random.fold_in(jax.random.fold_in(key, 6), dim), (shards_of,), jnp.float32, least / len(pieces), largest / len(pieces))
        gain = gain * jnp.repeat(jnp.exp(steps), shape[dim] // shards_of).reshape((-1,) + (1,) * (len(shape) - 1 - dim))
    return gain


def bell_draw(key, shape, width, limit, cuts=(), held_as=jnp.bfloat16):
    entries = width * jax.random.normal(key, shape, jnp.float32)
    if cuts:
        entries = entries * block_levels(key, shape, cuts, -0.22, 0.18)
    return jnp.clip(entries, -limit, limit).astype(held_as)


def setup_inputs(seed: int = 0, part: int = 0) -> dict:
    arg_keys = jax.random.split(jax.random.key(seed), 12)
    own_keys = jax.random.split(jax.random.fold_in(arg_keys[11], part), 12)
    return {
        "positions": draw_positions(jax.random.fold_in(jax.random.fold_in(arg_keys[11], part), 71), part),
        "strengths": bell_draw(own_keys[1], (NBLK, 3, BLK), 2.0, 12.0, ((0, 16),), jnp.float32),
        "history": bell_draw(own_keys[2], (NBLK, 2, 3, BLK), 0.7, 5.0, ((0, 16),), jnp.float32),
        "move_list": draw_move_list(jax.random.fold_in(jax.random.fold_in(arg_keys[11], part), 71), part),
        "age_slot": draw_age_slot(jax.random.fold_in(jax.random.fold_in(arg_keys[11], part), 71), part),
        "fetch_list": draw_fetch_list(jax.random.fold_in(jax.random.fold_in(arg_keys[11], part), 71), part),
        "tile_slot": draw_tile_slot(jax.random.fold_in(jax.random.fold_in(arg_keys[11], part), 71), part),
        "tile_count": draw_tile_count(jax.random.fold_in(jax.random.fold_in(arg_keys[11], part), 71), part),
        "blade_id": plant(jax.random.randint(own_keys[8], (NBLK, BLK), 0, ROTORS * BLADES), jax.random.fold_in(own_keys[8], 1), 0, (ROTORS * BLADES) - 1).astype(jnp.int32),
        "hub_centre": bell_draw(own_keys[9], (ROTORS, 3), 2.0, 8.0, (), jnp.float32),
        "azimuth": jnp.clip(jax.random.uniform(own_keys[10], (ROTORS,), jnp.float32, -3.140625, 3.140625), -3.140625, 3.140625),
    }


core_square = 0.05
time_step = 0.05


def cross_product(first, second):
    return jnp.stack([first[..., 1, :] * second[..., 2, :] - first[..., 2, :] * second[..., 1, :],
                      first[..., 2, :] * second[..., 0, :] - first[..., 0, :] * second[..., 2, :],
                      first[..., 0, :] * second[..., 1, :] - first[..., 1, :] * second[..., 0, :]], axis=-2)


def induced(target, source_pos, source_table, tile_mask):
    dist_sq = jnp.zeros((source_pos.shape[0], target.shape[-1], source_pos.shape[-1]), jnp.float32)
    for component in range(3):
        gap = target[component][None, :, None] - source_pos[:, component][:, None, :]
        dist_sq = dist_sq + gap * gap
    weight = tile_mask[:, None, None] * (dist_sq + core_square) ** -1.5
    summed = jnp.einsum("kij,kcj->ci", weight, source_table, precision=lax.Precision.HIGHEST)
    return (cross_product(target, summed[:3]) - summed[3:]) / (4.0 * math.pi)


def reference(positions, strengths, history, move_list, age_slot, fetch_list, tile_slot, tile_count, blade_id, hub_centre, azimuth):
    block_total = positions.shape[0]
    table = jnp.concatenate([strengths, cross_product(positions, strengths)], axis=1)
    device = (jnp.arange(block_total, dtype=jnp.int32) // NB_DEV)[:, None]
    owner = tile_slot // RCAP
    within = tile_slot % RCAP
    source = (owner * NB_DEV + fetch_list[device, owner, within]).astype(jnp.int32)
    tile_mask = (jnp.arange(KMAX, dtype=jnp.int32)[None, :] < tile_count[:, None]).astype(jnp.float32)

    def one_target(packed):
        target, sources, weights = packed
        return induced(target, positions[sources], table[sources], weights)

    velocity = lax.map(one_target, (positions, source, tile_mask), batch_size=8)
    moved = jnp.zeros_like(history).at[move_list].set(history)
    new_positions = positions + time_step * (23.0 * velocity - 16.0 * moved[:, 0] + 5.0 * moved[:, 1]) / 12.0
    new_history = jnp.stack([velocity, moved[:, 0]], axis=1)
    aged = jnp.zeros_like(new_positions).at[age_slot].set(new_positions)
    blade_angle = (azimuth[:, None] + 2.0 * math.pi * jnp.arange(BLADES, dtype=jnp.float32)[None, :] / BLADES).reshape(-1)
    angle = blade_angle[blade_id]
    rotor = blade_id // BLADES
    centre = hub_centre[rotor]
    first = aged[:, 0] - centre[..., 0]
    second = aged[:, 1] - centre[..., 1]
    third = aged[:, 2] - centre[..., 2]
    cosine = jnp.cos(angle)
    sine = jnp.sin(angle)
    frame = jnp.stack([cosine * first + sine * second, cosine * second - sine * first, third], axis=1)
    return new_positions, new_history, frame
```

```python
import functools
import math

import jax
import jax.numpy as jnp
from jax import lax
from jax.experimental import pallas as pl
from jax.experimental.pallas import tpu as pltpu
from jax.sharding import PartitionSpec as P

ROTORS = 6
BLADES = 3

core_square = 0.05
time_step = 0.05

LANES = 128
FEATURES = 32
UNROLL = 16
BF = jnp.bfloat16
F32 = jnp.float32

SMEM = pl.BlockSpec(memory_space=pltpu.SMEM)
VMEM = pl.BlockSpec(memory_space=pltpu.VMEM)


def params(limit=48 << 20):
    return pltpu.CompilerParams(vmem_limit_bytes=limit)


def split3(value):
    high = value.astype(BF).astype(F32)
    rest = value - high
    middle = rest.astype(BF).astype(F32)
    return high, middle, rest - middle


def meta_kernel(blocks, boxes, rcap, cap, move, age, fetch, meta, move_place, age_place, fill):
    def clear(p, carry):
        for lane in range(rcap):
            meta[p, lane] = fetch[p, lane]
        for lane in range(2 * cap):
            meta[p, rcap + lane] = -1
        fill[p] = 0
        fill[boxes + p] = 0
        return carry

    lax.fori_loop(0, boxes, clear, 0)

    def place(g, carry):
        for source, first, target, lane in (
            (move, 0, move_place, rcap),
            (age, boxes, age_place, rcap + cap),
        ):
            block = source[g]
            box = lax.div(block, blocks)
            rank = fill[first + box]
            fill[first + box] = rank + 1
            meta[box, lane + rank] = block - box * blocks
            target[g] = box * 256 + rank
        return carry

    lax.fori_loop(0, blocks, place, 0)


def history_kernel(blocks, cap, place, history, packed):
    def one(g, carry):
        where = place[g]
        box = where >> 8
        rank = where & 255
        packed[box, pl.ds(rank, 3, stride=cap), :] = history[g, 0]
        packed[box, pl.ds(3 * cap + rank, 3, stride=cap), :] = history[g, 1]
        return carry

    lax.fori_loop(0, blocks, one, 0, unroll=4)


def list_kernel(blocks, kmax, slots, limit, tiles, slot_list, pair_list, used, totals,
                ranked, counted, ranked_s, counted_s, sems):
    groups = slots // LANES
    lane = lax.broadcasted_iota(jnp.int32, (blocks, LANES), 1)
    row = lax.broadcasted_iota(jnp.int32, (blocks, LANES), 0)
    before = (
        lax.broadcasted_iota(jnp.int32, (blocks, blocks), 1)
        < lax.broadcasted_iota(jnp.int32, (blocks, blocks), 0)
    ).astype(BF)
    for group in range(groups):
        count = jnp.zeros((blocks, LANES), jnp.int32)
        for k in range(kmax):
            count = count + jnp.where(tiles[:, k : k + 1] == lane + group * LANES, 1, 0)
        present = (count > 0).astype(F32)
        rank = jnp.dot(before, present.astype(BF), preferred_element_type=F32).astype(jnp.int32)
        rank = jnp.where(count > 0, rank, -1)
        entry = row + count * 256
        number = jnp.sum(present, axis=0, keepdims=True).astype(jnp.int32)
        counted[group * 8 : (group + 1) * 8, :] = jnp.broadcast_to(number, (8, LANES))

        def fill(r, carry):
            found = jnp.sum(jnp.where(rank == r, entry, 0), axis=0, keepdims=True)
            ranked[pl.ds(group * blocks + r, 1), :] = found
            return carry

        lax.fori_loop(0, ((jnp.max(number) + 1) >> 1) << 1, fill, 0)
    copies = [
        pltpu.make_async_copy(ranked, ranked_s, sems.at[0]),
        pltpu.make_async_copy(counted, counted_s, sems.at[1]),
    ]
    for copy in copies:
        copy.start()
    for copy in copies:
        copy.wait()

    carry = (0, 0)
    for group in range(groups):

        def flatten(col, carry):
            filled, users = carry
            half = (counted_s[group * 8, col] + 1) >> 1
            slot = group * LANES + col
            used[users] = slot

            def pair(t, carry):
                first = ranked_s[group * blocks + 2 * t, col]
                second = ranked_s[group * blocks + 2 * t + 1, col]
                slot_list[filled + t] = slot
                pair_list[filled + t] = first + second * 65536
                return carry

            lax.fori_loop(0, half, pair, 0)
            return filled + half, users + jnp.where(half > 0, 1, 0)

        carry = lax.fori_loop(0, LANES, flatten, carry)
    filled, users = carry
    for t in range(UNROLL):
        slot_list[filled + t] = used[0]
        pair_list[filled + t] = 0
    for t in range(8):
        used[users + t] = used[0]
    totals[0] = lax.div(filled + (UNROLL - 1), UNROLL)
    totals[1] = (users + 7) >> 3


def target_kernel(blocks, positions, blade, hub, azimuth, feats, centre, tables, stage):
    total = jnp.zeros((3, LANES), F32)
    for b in range(blocks):
        total = total + positions[b]
    middle = jnp.sum(total, axis=1, keepdims=True) / (blocks * LANES)
    middle = jnp.broadcast_to(middle, (3, LANES))
    centre[0:3, :] = middle
    ones = jnp.ones((8, LANES), F32)
    pad = jnp.zeros((FEATURES - 24, LANES), F32)
    for group in range(blocks // 8):
        at = [
            positions[group * 8 : group * 8 + 8, axis, :] - middle[axis : axis + 1, :]
            for axis in range(3)
        ]
        norm = split3(at[0] * at[0] + at[1] * at[1] + at[2] * at[2] + core_square)
        parts = [split3(-2.0 * value) for value in at]
        rows = []
        for piece in (0, 1, 2, 0, 1, 0):
            rows += [parts[axis][piece] for axis in range(3)]
        rows += [ones, ones, ones, norm[0], norm[1], norm[2]]
        base = (group % 2) * 24 * 8
        for f, value in enumerate(rows):
            stage[base + f * 8 : base + f * 8 + 8, :] = value
        for t in range(8):
            picked = stage[pl.ds(base + t, 24, stride=8), :]
            feats[group * 8 + t] = jnp.concatenate([picked, pad], axis=0).astype(BF)
    lane = lax.broadcasted_iota(jnp.int32, (8, LANES), 1)
    angle = jnp.zeros((8, LANES), F32)
    hubs = [jnp.zeros((8, LANES), F32) for _ in range(3)]
    for q in range(ROTORS * BLADES):
        turn = F32(2.0 * math.pi) * F32(q % BLADES) / F32(BLADES)
        angle = jnp.where(lane == q, azimuth[q // BLADES] + turn, angle)
        for axis in range(3):
            hubs[axis] = jnp.where(lane == q, hub[q // BLADES, axis], hubs[axis])
    sources = [jnp.cos(angle), jnp.sin(angle)] + hubs
    for group in range(blocks // 8):
        index = blade[group * 8 : group * 8 + 8, :]
        for n, source in enumerate(sources):
            tables[n, group * 8 : group * 8 + 8, :] = jnp.take_along_axis(source, index, axis=1)


def answer_kernel(boxes, rcap, asked, positions, strengths, packed):
    def one(p, carry):
        for i in range(rcap):
            block = jnp.maximum(asked[p, i], 0)
            packed[p, pl.ds(i, 3, stride=rcap), :] = positions[block]
            packed[p, pl.ds(3 * rcap + i, 3, stride=rcap), :] = strengths[block]
        return carry

    lax.fori_loop(0, boxes, one, 0)


def arrival_kernel(boxes, rcap, cap, blocks, labels, moved_from, aged_from):
    def one(p, carry):
        for rank in range(cap):
            for target, lane in ((moved_from, rcap), (aged_from, rcap + cap)):
                label = labels[p, lane + rank]
                target[jnp.where(label < 0, blocks, label)] = p * 256 + rank
        return carry

    lax.fori_loop(0, boxes, one, 0)


def velocity_kernel(blocks, boxes, rcap, cap, slot_list, pair_list, used, totals, moved_from,
                    age_place, fetched, arrived, positions, targets, centre,
                    new_positions, new_history, outgoing,
                    stage, table_stage, feats, tables, sums, speed):
    rows = 24 * 8
    ones = jnp.ones((8, LANES), F32)
    zeros = jnp.zeros((8, LANES), F32)

    def prepare(o, carry):
        at = [
            fetched[o, axis * rcap : (axis + 1) * rcap, :] - centre[axis : axis + 1, :]
            for axis in range(3)
        ]
        gamma = [fetched[o, (3 + axis) * rcap : (4 + axis) * rcap, :] for axis in range(3)]
        parts = [split3(value) for value in at]
        norm = split3(at[0] * at[0] + at[1] * at[1] + at[2] * at[2])
        values = []
        for piece in (0, 0, 0, 1, 1, 2):
            values += [parts[axis][piece] for axis in range(3)]
        values += [norm[0], norm[1], norm[2], ones, ones, ones]
        for f, value in enumerate(values):
            stage[o, f * 8 : f * 8 + 8, :] = value
        for axis in range(3):
            left, right = (axis + 1) % 3, (axis + 2) % 3
            table_stage[o, axis * 8 : axis * 8 + 8, :] = gamma[axis]
            table_stage[o, (3 + axis) * 8 : (4 + axis) * 8, :] = (
                at[left] * gamma[right] - at[right] * gamma[left]
            )
        table_stage[o, 48:56, :] = zeros
        table_stage[o, 56:64, :] = zeros
        return carry

    lax.fori_loop(0, boxes, prepare, 0)
    identity = (
        lax.broadcasted_iota(jnp.int32, (LANES, LANES), 0)
        == lax.broadcasted_iota(jnp.int32, (LANES, LANES), 1)
    ).astype(BF)
    pad = jnp.zeros((FEATURES - 24, LANES), F32)

    def build(it, carry):
        for u in range(8):
            slot = used[it * 8 + u]
            o = slot >> 3
            i = slot & 7
            picked = jnp.concatenate([stage[o, pl.ds(i, 24, stride=8), :], pad], axis=0)
            turned = lax.dot_general(
                identity, picked.astype(BF), (((1,), (1,)), ((), ())), preferred_element_type=F32
            )
            feats[slot] = turned.astype(BF)
            table = table_stage[o, pl.ds(i, 8, stride=8), :]
            high = table.astype(BF).astype(F32)
            left = jnp.concatenate([high, table - high], axis=0)
            right = jnp.concatenate([high, zeros], axis=0)
            tables[slot] = jnp.concatenate([left, right], axis=1).astype(BF)
        return carry

    lax.fori_loop(0, totals[1], build, 0)
    sums[...] = jnp.zeros_like(sums)

    def accumulate(it, carry):
        found = []
        for u in range(UNROLL):
            slot = slot_list[it * UNROLL + u]
            pair = pair_list[it * UNROLL + u]
            first = pair & 255
            second = (pair >> 16) & 255
            both = jnp.concatenate([targets[first], targets[second]], axis=1)
            inverse = lax.rsqrt(jnp.dot(feats[slot], both, preferred_element_type=F32))
            weight = inverse * inverse * inverse
            high = weight.astype(BF)
            low = (weight - high.astype(F32)).astype(BF)
            summed = jnp.dot(
                tables[slot], jnp.concatenate([high, low], axis=0), preferred_element_type=F32
            )
            times = (((pair >> 8) & 255).astype(F32), (pair >> 24).astype(F32))
            found.append((first, second, times, summed))
        for first, second, times, summed in found:
            for target, factor, part in (
                (first, times[0], summed[:, :LANES]),
                (second, times[1], summed[:, LANES:]),
            ):
                at = pl.ds(pl.multiple_of(target * 16, 16), 16)
                sums[at, :] = sums[at, :] + factor * part
        return carry

    lax.fori_loop(0, totals[0], accumulate, 0)

    scale = 1.0 / (4.0 * math.pi)
    for group in range(blocks // 8):
        first = group * 8
        total = [
            sums[pl.ds(first * 16 + f, 8, stride=16), :]
            + sums[pl.ds(first * 16 + 8 + f, 8, stride=16), :]
            for f in range(6)
        ]
        at = [positions[first : first + 8, axis, :] - centre[axis : axis + 1, :] for axis in range(3)]
        for axis in range(3):
            left, right = (axis + 1) % 3, (axis + 2) % 3
            speed[axis * blocks + first : axis * blocks + first + 8, :] = scale * (
                at[left] * total[right] - at[right] * total[left] - total[3 + axis]
            )
    unused = jnp.zeros((3 * cap, LANES), F32)

    def clear(p, carry):
        outgoing[p] = unused
        return carry

    lax.fori_loop(0, boxes, clear, 0)

    def finish(b, carry):
        where = moved_from[b]
        box = where >> 8
        rank = where & 255
        recent = arrived[box, pl.ds(rank, 3, stride=cap), :]
        older = arrived[box, pl.ds(3 * cap + rank, 3, stride=cap), :]
        now = speed[pl.ds(b, 3, stride=blocks), :]
        stepped = positions[b] + time_step * (23.0 * now - 16.0 * recent + 5.0 * older) / 12.0
        new_positions[b] = stepped
        new_history[b, 0] = now
        new_history[b, 1] = recent
        out = age_place[b]
        outgoing[out >> 8, pl.ds(out & 255, 3, stride=cap), :] = stepped
        return carry

    lax.fori_loop(0, blocks, finish, 0, unroll=4)


def frame_kernel(blocks, cap, aged_from, arrived, tables, frame):
    def one(b, carry):
        where = aged_from[b]
        aged = arrived[where >> 8, pl.ds(where & 255, 3, stride=cap), :]
        cosine, sine, hub0, hub1, hub2 = [tables[n, pl.ds(b, 1), :] for n in range(5)]
        first = aged[0:1] - hub0
        second = aged[1:2] - hub1
        frame[b, 0:1, :] = cosine * first + sine * second
        frame[b, 1:2, :] = cosine * second - sine * first
        frame[b, 2:3, :] = aged[2:3] - hub2
        return carry

    lax.fori_loop(0, blocks, one, 0, unroll=8)


def swap(values):
    return lax.all_to_all(values, "box", split_axis=0, concat_axis=0, tiled=True)


def body(
    positions,
    strengths,
    history,
    move_list,
    age_slot,
    fetch_list,
    tile_slot,
    tile_count,
    blade_id,
    hub_centre,
    azimuth,
):
    blocks = positions.shape[0]
    boxes = lax.axis_size("box")
    rcap = fetch_list.shape[2]
    kmax = tile_slot.shape[1]
    cap = 2 * blocks // boxes
    slots = boxes * rcap
    limit = (blocks * kmax + slots) // 2 + 2 * UNROLL

    def shape(dims, dtype=F32):
        return jax.ShapeDtypeStruct(dims, dtype)

    meta, move_place, age_place = pl.pallas_call(
        functools.partial(meta_kernel, blocks, boxes, rcap, cap),
        in_specs=[SMEM] * 3,
        out_specs=[SMEM] * 3,
        out_shape=[
            shape((boxes, LANES), jnp.int32),
            shape((blocks,), jnp.int32),
            shape((blocks,), jnp.int32),
        ],
        scratch_shapes=[pltpu.SMEM((2 * boxes,), jnp.int32)],
        name="meta",
    )(move_list, age_slot, fetch_list[0])
    labels = swap(meta)
    packed_history = pl.pallas_call(
        functools.partial(history_kernel, blocks, cap),
        in_specs=[SMEM, VMEM],
        out_specs=VMEM,
        out_shape=shape((boxes, 6 * cap, LANES)),
        name="pack_history",
    )(move_place, history)
    tiles = jnp.where(
        jnp.arange(kmax, dtype=jnp.int32)[None, :] < tile_count[:, None], tile_slot, -1
    )
    groups = slots // LANES
    slot_list, pair_list, used, totals = pl.pallas_call(
        functools.partial(list_kernel, blocks, kmax, slots, limit),
        in_specs=[VMEM],
        out_specs=[SMEM] * 4,
        out_shape=[
            shape((limit,), jnp.int32),
            shape((limit,), jnp.int32),
            shape((slots + 8,), jnp.int32),
            shape((2,), jnp.int32),
        ],
        scratch_shapes=[
            pltpu.VMEM((groups * blocks, LANES), jnp.int32),
            pltpu.VMEM((groups * 8, LANES), jnp.int32),
            pltpu.SMEM((groups * blocks, LANES), jnp.int32),
            pltpu.SMEM((groups * 8, LANES), jnp.int32),
            pltpu.SemaphoreType.DMA((2,)),
        ],
        name="pair_list",
    )(tiles)
    targets, centre, tables = pl.pallas_call(
        functools.partial(target_kernel, blocks),
        in_specs=[VMEM, VMEM, SMEM, SMEM],
        out_specs=[VMEM] * 3,
        out_shape=[
            shape((blocks, FEATURES, LANES), BF),
            shape((8, LANES)),
            shape((5, blocks, LANES)),
        ],
        scratch_shapes=[pltpu.VMEM((2 * 24 * 8, LANES), F32)],
        name="target_features",
    )(positions, blade_id, hub_centre, azimuth)
    answers = pl.pallas_call(
        functools.partial(answer_kernel, boxes, rcap),
        in_specs=[SMEM, VMEM, VMEM],
        out_specs=VMEM,
        out_shape=shape((boxes, 6 * rcap, LANES)),
        name="answer",
    )(labels, positions, strengths)
    fetched = swap(answers)
    arrived = swap(packed_history)
    moved_from, aged_from = pl.pallas_call(
        functools.partial(arrival_kernel, boxes, rcap, cap, blocks),
        in_specs=[SMEM],
        out_specs=[SMEM] * 2,
        out_shape=[shape((blocks + 1,), jnp.int32)] * 2,
        name="arrivals",
    )(labels)
    new_positions, new_history, outgoing = pl.pallas_call(
        functools.partial(velocity_kernel, blocks, boxes, rcap, cap),
        in_specs=[SMEM] * 6 + [VMEM] * 5,
        out_specs=[VMEM] * 3,
        out_shape=[
            shape((blocks, 3, LANES)),
            shape((blocks, 2, 3, LANES)),
            shape((boxes, 3 * cap, LANES)),
        ],
        scratch_shapes=[
            pltpu.VMEM((boxes, 24 * 8, LANES), F32),
            pltpu.VMEM((boxes, 64, LANES), F32),
            pltpu.VMEM((slots, LANES, FEATURES), BF),
            pltpu.VMEM((slots, 16, 2 * LANES), BF),
            pltpu.VMEM((blocks * 16, LANES), F32),
            pltpu.VMEM((3 * blocks, LANES), F32),
        ],
        compiler_params=params(),
        name="velocity",
    )(
        slot_list, pair_list, used, totals, moved_from, age_place,
        fetched, arrived, positions, targets, centre,
    )
    aged = swap(outgoing)
    frame = pl.pallas_call(
        functools.partial(frame_kernel, blocks, cap),
        in_specs=[SMEM, VMEM, VMEM],
        out_specs=VMEM,
        out_shape=shape((blocks, 3, LANES)),
        name="frame",
    )(aged_from, aged, tables)
    return new_positions, new_history, frame


def solution(mesh):
    split = ("cases", "box")
    placed = (
        P(split, None, None),
        P(split, None, None),
        P(split, None, None, None),
        P(split),
        P(split),
        P(split, None, None),
        P(split, None),
        P(split),
        P(split, None),
        P("cases", None),
        P("cases"),
    )
    return jax.shard_map(
        body,
        mesh=mesh,
        in_specs=placed,
        out_specs=(P(split, None, None), P(split, None, None, None), P(split, None, None)),
        check_vma=False,
    )
```

```python
import functools
import math

import jax
import jax.numpy as jnp
from jax import lax
from jax.experimental import pallas as pl
from jax.experimental.pallas import tpu as pltpu
from jax.sharding import PartitionSpec as P

ROTORS = 6
BLADES = 3

core_square = 0.05
time_step = 0.05

LANES = 128
UNROLL = 32
BUILD = 8
BF = jnp.bfloat16
F32 = jnp.float32
I32 = jnp.int32

SMEM = pl.BlockSpec(memory_space=pltpu.SMEM)
VMEM = pl.BlockSpec(memory_space=pltpu.VMEM)


def split3(value):
    high = value.astype(BF).astype(F32)
    rest = value - high
    middle = rest.astype(BF).astype(F32)
    return high, middle, rest - middle


def iota(dims, axis):
    return lax.broadcasted_iota(I32, dims, axis)


def meta_kernel(blocks, boxes, rcap, cap, move, age, fetch, meta, move_place, age_place, fill):
    def ask(p, carry):
        for lane in range(rcap):
            meta[p, lane] = fetch[lane, p]
        fill[p] = 0
        fill[boxes + p] = 0
        return carry

    lax.fori_loop(0, boxes, ask, 0, unroll=4)

    def place(g, carry):
        for source, first, target, lane in (
            (move, 0, move_place, rcap),
            (age, boxes, age_place, rcap + cap),
        ):
            block = source[g]
            box = lax.div(block, blocks)
            rank = fill[first + box]
            fill[first + box] = rank + 1
            meta[box, lane + rank] = block - box * blocks
            target[g] = box * 256 + rank
        return carry

    lax.fori_loop(0, blocks, place, 0, unroll=4)

    def number(p, carry):
        meta[p, rcap + 2 * cap] = fill[p]
        meta[p, rcap + 2 * cap + 1] = fill[boxes + p]
        return carry

    lax.fori_loop(0, boxes, number, 0, unroll=4)


def history_kernel(blocks, boxes, rcap, cap, place, labels, history, packed, moved_from, aged_from):
    def one(g, carry):
        where = place[g]
        box = where >> 8
        rank = where & 255
        for axis in range(3):
            packed[box, pl.ds(axis * cap + rank, 2, stride=3 * cap), :] = history[g, axis]
        return carry

    lax.fori_loop(0, blocks, one, 0, unroll=4)

    def peer(p, carry):
        for target, lane, number in ((moved_from, rcap, 0), (aged_from, rcap + cap, 1)):

            def label(rank, carry):
                target[labels[p, lane + rank]] = p * 256 + rank
                return carry

            lax.fori_loop(0, labels[p, rcap + 2 * cap + number], label, 0)
        return carry

    lax.fori_loop(0, boxes, peer, 0)


def plan_rows(slots, most):
    chunks = (most + LANES - 1) // LANES
    users = (slots + BUILD + LANES - 1) // LANES
    return chunks, users, (chunks + users + 2 + 7) // 8 * 8


def plan_kernel(blocks, kmax, slots, most, tiles, count, plan, ranked):
    half = kmax
    chunks, users, rows = plan_rows(slots, most)
    slot = iota((slots, blocks), 0)
    times = jnp.zeros((slots, blocks), I32)
    for k in range(kmax):
        named = jnp.where(count[...] > k, tiles[k : k + 1, :], -1)
        times = times + jnp.where(slot == named, 1, 0)
    present = jnp.where(times > 0, 1.0, 0.0)
    inner = jnp.where(iota((blocks, blocks), 0) < iota((blocks, blocks), 1), 1.0, 0.0)
    rank = jnp.dot(present.astype(BF), inner.astype(BF), preferred_element_type=F32)
    rank = jnp.where(times > 0, rank, -2.0)
    number = jnp.dot(
        present.astype(BF), jnp.ones((blocks, LANES), BF), preferred_element_type=F32
    ).astype(I32)
    pairs = (number + 1) >> 1
    outer = jnp.where(iota((slots, slots), 1) <= iota((slots, slots), 0), 1.0, 0.0).astype(BF)
    ends = jnp.dot(outer, pairs.astype(F32).astype(BF), preferred_element_type=F32).astype(I32)
    used = jnp.where(number > 0, 1.0, 0.0).astype(BF)
    tally = jnp.dot(outer, used, preferred_element_type=F32).astype(I32)
    total = ends[slots - 1 : slots, :]
    live = tally[slots - 1 : slots, :]
    opening = jnp.sum(jnp.where(tally <= 0, 1, 0), axis=0, keepdims=True)
    lane = iota((1, LANES), 1)
    for chunk in range(chunks):
        spot = lane + chunk * LANES
        past = ends <= spot
        source = jnp.sum(jnp.where(past, 1, 0), axis=0, keepdims=True)
        start = jnp.max(jnp.where(past, ends, 0), axis=0, keepdims=True)
        word = jnp.where(spot < total, source + (spot - start) * 65536, opening + half * 65536)
        plan[chunk : chunk + 1, :] = word
    for chunk in range(users):
        spot = lane + chunk * LANES
        source = jnp.sum(jnp.where(tally <= spot, 1, 0), axis=0, keepdims=True)
        plan[chunks + chunk : chunks + chunk + 1, :] = jnp.where(spot < live, source, opening)
    plan[rows - 2 : rows - 1, :] = (total + (UNROLL - 1)) >> (UNROLL.bit_length() - 1)
    plan[rows - 1 : rows, :] = (live + (BUILD - 1)) >> (BUILD.bit_length() - 1)
    limit = jnp.max(pairs)
    for group in range(slots // LANES):
        at = slice(group * LANES, (group + 1) * LANES)
        wide = [
            jnp.concatenate([value, jnp.zeros((LANES, LANES - blocks), F32)], axis=1).T[:blocks]
            for value in (rank[at], times[at].astype(F32))
        ]
        position = wide[0].astype(I32)
        entry = iota((blocks, LANES), 0) + wide[1].astype(I32) * 256
        entry = jnp.where((position & 1) == 1, entry * 65536, entry)
        position = position >> 1
        first = group * (half + 8)
        ranked[first + half : first + half + 8, :] = jnp.zeros((8, LANES), I32)

        def fill(t, carry):
            found = jnp.sum(jnp.where(position == t, entry, 0), axis=0, keepdims=True)
            ranked[pl.ds(first + t, 1), :] = found
            return carry

        lax.fori_loop(0, limit, fill, 0)


def target_kernel(blocks, positions, blade, hub, azimuth, feats, centre, tables, stage):
    middle = [
        jnp.sum(positions[axis * blocks : (axis + 1) * blocks, :], axis=(0, 1), keepdims=True)
        / (blocks * LANES)
        for axis in range(3)
    ]
    for axis in range(3):
        centre[axis : axis + 1, :] = jnp.broadcast_to(middle[axis], (1, LANES))
    ones = jnp.ones((8, LANES), F32)
    pad = jnp.zeros((LANES - 24, LANES), F32)
    for group in range(blocks // 8):
        first = group * 8
        at = [
            positions[axis * blocks + first : axis * blocks + first + 8, :] - middle[axis]
            for axis in range(3)
        ]
        norm = split3(at[0] * at[0] + at[1] * at[1] + at[2] * at[2] + core_square)
        parts = [split3(-2.0 * value) for value in at]
        rows = []
        for piece in (0, 1, 2, 0, 1, 0):
            rows += [parts[axis][piece] for axis in range(3)]
        rows += [ones, ones, ones, norm[0], norm[1], norm[2]]
        base = (group % 2) * 24 * 8
        for f, value in enumerate(rows):
            stage[base + f * 8 : base + f * 8 + 8, :] = value
        for t in range(8):
            picked = stage[pl.ds(base + t, 24, stride=8), :]
            feats[first + t] = jnp.concatenate([picked, pad], axis=0).astype(BF)
    lane = iota((8, LANES), 1)
    angle = jnp.zeros((8, LANES), F32)
    hubs = [jnp.zeros((8, LANES), F32) for _ in range(3)]
    for q in range(ROTORS * BLADES):
        turn = F32(2.0 * math.pi) * F32(q % BLADES) / F32(BLADES)
        angle = jnp.where(lane == q, azimuth[q // BLADES] + turn, angle)
        for axis in range(3):
            hubs[axis] = jnp.where(lane == q, hub[axis, q // BLADES], hubs[axis])
    sources = [jnp.cos(angle), jnp.sin(angle)] + hubs
    for group in range(blocks // 8):
        index = blade[group * 8 : group * 8 + 8, :]
        for n, source in enumerate(sources):
            tables[n, group * 8 : group * 8 + 8, :] = jnp.take_along_axis(source, index, axis=1)


def answer_kernel(blocks, boxes, rcap, asked, positions, strengths, packed):
    def one(p, carry):
        for i in range(rcap):
            block = jnp.maximum(asked[p, i], 0)
            packed[p, pl.ds(i, 3, stride=rcap), :] = positions[pl.ds(block, 3, stride=blocks), :]
            packed[p, pl.ds(3 * rcap + i, 3, stride=rcap), :] = strengths[
                pl.ds(block, 3, stride=blocks), :
            ]
        return carry

    lax.fori_loop(0, boxes, one, 0)


def velocity_kernel(blocks, boxes, rcap, slots, half, most, plan, ranked, fetched, positions,
                    targets, centre, speed, stage, table_stage, feats, tables, sums0, sums1, held):
    chunks, _, rows = plan_rows(slots, most)
    ones = jnp.ones((8, LANES), F32)
    zeros = jnp.zeros((8, LANES), F32)

    def prepare(o, carry):
        at = [
            fetched[o, axis * rcap : (axis + 1) * rcap, :] - centre[axis : axis + 1, :]
            for axis in range(3)
        ]
        gamma = [fetched[o, (3 + axis) * rcap : (4 + axis) * rcap, :] for axis in range(3)]
        parts = [split3(value) for value in at]
        norm = split3(at[0] * at[0] + at[1] * at[1] + at[2] * at[2])
        values = []
        for piece in (0, 0, 0, 1, 1, 2):
            values += [parts[axis][piece] for axis in range(3)]
        values += [norm[0], norm[1], norm[2], ones, ones, ones]
        for f, value in enumerate(values):
            stage[o, f * 8 : f * 8 + 8, :] = value
        for axis in range(3):
            left, right = (axis + 1) % 3, (axis + 2) % 3
            table_stage[o, axis * 8 : axis * 8 + 8, :] = gamma[axis]
            table_stage[o, (3 + axis) * 8 : (4 + axis) * 8, :] = (
                at[left] * gamma[right] - at[right] * gamma[left]
            )
        table_stage[o, 48:56, :] = zeros
        table_stage[o, 56:64, :] = zeros
        return carry

    lax.fori_loop(0, boxes, prepare, 0, unroll=2)
    identity = jnp.where(
        iota((LANES, LANES), 0) == iota((LANES, LANES), 1), 1.0, 0.0
    ).astype(BF)
    pad = jnp.zeros((LANES - 24, LANES), F32)

    def build(it, carry):
        for u in range(BUILD):
            at = it * BUILD + u
            slot = plan[chunks + (at >> 7), at & 127]
            o = slot >> 3
            i = slot & 7
            picked = jnp.concatenate([stage[o, pl.ds(i, 24, stride=8), :], pad], axis=0)
            turned = lax.dot_general(
                identity, picked.astype(BF), (((1,), (1,)), ((), ())), preferred_element_type=F32
            )
            feats[slot] = turned.astype(BF)
            table = table_stage[o, pl.ds(i, 8, stride=8), :]
            high = table.astype(BF).astype(F32)
            left = jnp.concatenate([high, table - high], axis=0)
            right = jnp.concatenate([high, zeros], axis=0)
            tables[slot] = jnp.concatenate([left, right], axis=1).astype(BF)
        return carry

    lax.fori_loop(0, plan[rows - 1, 0], build, 0)
    sums0[...] = jnp.zeros_like(sums0)
    sums1[...] = jnp.zeros_like(sums1)
    held[...] = jnp.zeros_like(held)

    def named(it):
        found = []
        for u in range(UNROLL):
            at = it * UNROLL + u
            word = plan[at >> 7, at & 127]
            slot = word & 65535
            row = word >> 16
            if slots > LANES:
                row = row + (slot >> 7) * (half + 8)
            found.append((slot, ranked[row, slot & 127]))
        return found

    def flush(it):
        for u, (_, pair) in enumerate(named(it)):
            for sums, word, part in (
                (sums0, pair & 65535, held[u, :, :LANES]),
                (sums1, pair >> 16, held[u, :, LANES:]),
            ):
                at = pl.ds(pl.multiple_of((word & 255) * 8, 8), 8)
                sums[at, :] = sums[at, :] + (word >> 8).astype(F32) * part

    def accumulate(it, carry):
        flush(jnp.maximum(it - 1, 0))
        for u, (slot, pair) in enumerate(named(it)):
            both = jnp.concatenate([targets[pair & 255], targets[(pair >> 16) & 255]], axis=1)
            inverse = lax.rsqrt(jnp.dot(feats[slot], both, preferred_element_type=F32))
            weight = inverse * inverse * inverse
            high = weight.astype(BF)
            low = (weight - high.astype(F32)).astype(BF)
            summed = jnp.dot(
                tables[slot], jnp.concatenate([high, low], axis=0), preferred_element_type=F32
            )
            held[u] = summed[:8] + summed[8:]
        return carry

    number = plan[rows - 2, 0]
    lax.fori_loop(0, number, accumulate, 0)
    flush(number - 1)

    scale = 1.0 / (4.0 * math.pi)
    for group in range(blocks // 8):
        first = group * 8
        total = [
            sums0[pl.ds(first * 8 + f, 8, stride=8), :] + sums1[pl.ds(first * 8 + f, 8, stride=8), :]
            for f in range(6)
        ]
        at = [
            positions[axis * blocks + first : axis * blocks + first + 8, :]
            - centre[axis : axis + 1, :]
            for axis in range(3)
        ]
        for axis in range(3):
            left, right = (axis + 1) % 3, (axis + 2) % 3
            speed[axis * blocks + first : axis * blocks + first + 8, :] = scale * (
                at[left] * total[right] - at[right] * total[left] - total[3 + axis]
            )


def step_kernel(blocks, boxes, cap, moved_from, age_place, arrived, positions, speed,
                new_positions, new_history, outgoing):
    unused = jnp.zeros((3 * cap, LANES), F32)

    def clear(p, carry):
        outgoing[p] = unused
        return carry

    lax.fori_loop(0, boxes, clear, 0)

    def finish(b, carry):
        where = moved_from[b]
        box = where >> 8
        rank = where & 255
        recent = arrived[box, pl.ds(rank, 3, stride=cap), :]
        older = arrived[box, pl.ds(3 * cap + rank, 3, stride=cap), :]
        rows = pl.ds(b, 3, stride=blocks)
        now = speed[rows, :]
        stepped = positions[rows, :] + time_step * (23.0 * now - 16.0 * recent + 5.0 * older) / 12.0
        new_positions[rows, :] = stepped
        for axis in range(3):
            new_history[b, axis, 0:1, :] = now[axis : axis + 1]
            new_history[b, axis, 1:2, :] = recent[axis : axis + 1]
        out = age_place[b]
        outgoing[out >> 8, pl.ds(out & 255, 3, stride=cap), :] = stepped
        return carry

    lax.fori_loop(0, blocks, finish, 0, unroll=4)


def frame_kernel(blocks, cap, aged_from, arrived, tables, frame):
    def one(b, carry):
        where = aged_from[b]
        aged = arrived[where >> 8, pl.ds(where & 255, 3, stride=cap), :]
        cosine, sine, hub0, hub1, hub2 = [tables[n, pl.ds(b, 1), :] for n in range(5)]
        first = aged[0:1] - hub0
        second = aged[1:2] - hub1
        frame[pl.ds(b, 1), :] = cosine * first + sine * second
        frame[pl.ds(blocks + b, 1), :] = cosine * second - sine * first
        frame[pl.ds(2 * blocks + b, 1), :] = aged[2:3] - hub2
        return carry

    lax.fori_loop(0, blocks, one, 0, unroll=8)


def swap(values):
    return lax.all_to_all(values, "box", split_axis=0, concat_axis=0, tiled=True)


def call(kernel, name, in_specs, outs, scratch=(), limit=None):
    several = isinstance(outs, list)
    listed = outs if several else [outs]
    specs = [spec for spec, _, _ in listed]
    shapes = [jax.ShapeDtypeStruct(dims, dtype) for _, dims, dtype in listed]
    return pl.pallas_call(
        kernel,
        in_specs=in_specs,
        out_specs=specs if several else specs[0],
        out_shape=shapes if several else shapes[0],
        scratch_shapes=list(scratch),
        compiler_params=pltpu.CompilerParams(vmem_limit_bytes=limit),
        name=name,
    )


def body(
    positions,
    strengths,
    history,
    move_list,
    age_slot,
    fetch_list,
    tile_slot,
    tile_count,
    blade_id,
    hub_centre,
    azimuth,
):
    blocks = positions.shape[0]
    boxes = lax.axis_size("box")
    rcap = fetch_list.shape[2]
    kmax = tile_slot.shape[1]
    cap = 2 * blocks // boxes
    slots = boxes * rcap
    most = (blocks * kmax + slots) // 2 + UNROLL
    chunks, users, rows = plan_rows(slots, most)
    groups = slots // LANES

    places = jnp.transpose(positions, (1, 0, 2)).reshape(3 * blocks, LANES)
    gammas = jnp.transpose(strengths, (1, 0, 2)).reshape(3 * blocks, LANES)
    past = jnp.transpose(history, (0, 2, 1, 3))

    meta, move_place, age_place = call(
        functools.partial(meta_kernel, blocks, boxes, rcap, cap),
        "meta",
        [SMEM] * 3,
        [(SMEM, (boxes, LANES), I32), (SMEM, (blocks,), I32), (SMEM, (blocks,), I32)],
        [pltpu.SMEM((2 * boxes,), I32)],
    )(move_list, age_slot, fetch_list[0].T)
    labels = swap(meta)
    plan, ranked = call(
        functools.partial(plan_kernel, blocks, kmax, slots, most),
        "plan",
        [VMEM] * 2,
        [(VMEM, (rows, LANES), I32), (VMEM, (groups * (kmax + 8), LANES), I32)],
    )(tile_slot.T, tile_count.reshape(1, blocks))
    targets, centre, tables = call(
        functools.partial(target_kernel, blocks),
        "target_features",
        [VMEM, VMEM, SMEM, SMEM],
        [(VMEM, (blocks, LANES, LANES), BF), (VMEM, (8, LANES), F32), (VMEM, (5, blocks, LANES), F32)],
        [pltpu.VMEM((2 * 24 * 8, LANES), F32)],
    )(places, blade_id, hub_centre.T, azimuth)
    labels, plan, ranked, targets, centre, tables = lax.optimization_barrier(
        (labels, plan, ranked, targets, centre, tables)
    )
    answers = call(
        functools.partial(answer_kernel, blocks, boxes, rcap),
        "answer",
        [SMEM, VMEM, VMEM],
        (VMEM, (boxes, 6 * rcap, LANES), F32),
    )(labels, places, gammas)
    late_labels, late_past, answers = lax.optimization_barrier((labels, past, answers))
    fetched = swap(answers)
    packed_history, moved_from, aged_from = call(
        functools.partial(history_kernel, blocks, boxes, rcap, cap),
        "pack_history",
        [SMEM, SMEM, VMEM],
        [(VMEM, (boxes, 6 * cap, LANES), F32), (SMEM, (blocks,), I32), (SMEM, (blocks,), I32)],
    )(move_place, late_labels, late_past)
    fetched, packed_history = lax.optimization_barrier((fetched, packed_history))
    arrived = swap(packed_history)
    speed = call(
        functools.partial(velocity_kernel, blocks, boxes, rcap, slots, kmax, most),
        "velocity",
        [SMEM] * 2 + [VMEM] * 4,
        (VMEM, (3 * blocks, LANES), F32),
        [
            pltpu.VMEM((boxes, 24 * 8, LANES), F32),
            pltpu.VMEM((boxes, 64, LANES), F32),
            pltpu.VMEM((slots, LANES, LANES), BF),
            pltpu.VMEM((slots, 16, 2 * LANES), BF),
            pltpu.VMEM((blocks * 8, LANES), F32),
            pltpu.VMEM((blocks * 8, LANES), F32),
            pltpu.VMEM((UNROLL, 8, 2 * LANES), F32),
        ],
        48 << 20,
    )(plan, ranked, fetched, places, targets, centre)
    new_positions, new_history, outgoing = call(
        functools.partial(step_kernel, blocks, boxes, cap),
        "step",
        [SMEM] * 2 + [VMEM] * 3,
        [
            (VMEM, (3 * blocks, LANES), F32),
            (VMEM, (blocks, 3, 2, LANES), F32),
            (VMEM, (boxes, 3 * cap, LANES), F32),
        ],
    )(moved_from, age_place, arrived, places, speed)
    aged = swap(outgoing)
    frame = call(
        functools.partial(frame_kernel, blocks, cap),
        "frame",
        [SMEM, VMEM, VMEM],
        (VMEM, (3 * blocks, LANES), F32),
    )(aged_from, aged, tables)

    def back(rows):
        return jnp.transpose(rows.reshape(3, blocks, LANES), (1, 0, 2))

    return back(new_positions), jnp.transpose(new_history, (0, 2, 1, 3)), back(frame)


def solution(mesh):
    split = ("cases", "box")
    placed = (
        P(split, None, None),
        P(split, None, None),
        P(split, None, None, None),
        P(split),
        P(split),
        P(split, None, None),
        P(split, None),
        P(split),
        P(split, None),
        P("cases", None),
        P("cases"),
    )
    return jax.shard_map(
        body,
        mesh=mesh,
        in_specs=placed,
        out_specs=(P(split, None, None), P(split, None, None, None), P(split, None, None)),
        check_vma=False,
    )
```

```python
import functools
import math

import jax
import jax.numpy as jnp
from jax import lax
from jax.experimental import pallas as pl
from jax.experimental.pallas import tpu as pltpu
from jax.sharding import PartitionSpec as P

ROTORS = 6
BLADES = 3

core_square = 0.05
time_step = 0.05

LANES = 128
FEATURES = 32
UNROLL = 32
BUILD = 8
BF = jnp.bfloat16
F32 = jnp.float32
I32 = jnp.int32

SMEM = pl.BlockSpec(memory_space=pltpu.SMEM)
VMEM = pl.BlockSpec(memory_space=pltpu.VMEM)
ANY = pl.BlockSpec(memory_space=pl.ANY)


def split3(value):
    high = value.astype(BF).astype(F32)
    rest = value - high
    middle = rest.astype(BF).astype(F32)
    return high, middle, rest - middle


def iota(dims, axis):
    return lax.broadcasted_iota(I32, dims, axis)


def meta_kernel(blocks, boxes, rcap, cap, move, age, fetch, meta, move_place, age_place, fill):
    def ask(p, carry):
        for lane in range(rcap):
            meta[p, lane] = fetch[lane, p]
        fill[p] = 0
        fill[boxes + p] = 0
        return carry

    lax.fori_loop(0, boxes, ask, 0, unroll=4)

    def place(g, carry):
        for source, first, target, lane in (
            (move, 0, move_place, rcap),
            (age, boxes, age_place, rcap + cap),
        ):
            block = source[g]
            box = lax.div(block, blocks)
            rank = fill[first + box]
            fill[first + box] = rank + 1
            meta[box, lane + rank] = block - box * blocks
            target[g] = box * 256 + rank
        return carry

    lax.fori_loop(0, blocks, place, 0, unroll=4)

    def number(p, carry):
        meta[p, rcap + 2 * cap] = fill[p]
        meta[p, rcap + 2 * cap + 1] = fill[boxes + p]
        return carry

    lax.fori_loop(0, boxes, number, 0, unroll=4)


def plan_rows(slots, most):
    chunks = (most + LANES - 1) // LANES
    users = (slots + BUILD + LANES - 1) // LANES
    return chunks, users, (2 * chunks + users + 3 + 7) // 8 * 8


def plan_kernel(blocks, kmax, rcap, cap, slots, most, place, history, tiles, count,
                message, plan, ranked, packed, sem):
    def one(g, carry):
        where = place[g]
        box = where >> 8
        rank = where & 255
        for axis in range(3):
            packed[box, pl.ds(axis * cap + rank, 2, stride=3 * cap), :] = history[g, axis]
        return carry

    lax.fori_loop(0, blocks, one, 0, unroll=8)
    sent = pltpu.make_async_copy(packed, message.at[:, pl.ds(6 * rcap, packed.shape[1]), :], sem)
    sent.start()
    half = kmax
    near = 2 * rcap
    chunks, users, rows = plan_rows(slots, most)
    turn = lax.axis_index("box") * rcap
    slot = iota((slots, blocks), 0) ^ turn
    times = jnp.zeros((slots, blocks), I32)
    for k in range(kmax):
        named = jnp.where(count[...] > k, tiles[k : k + 1, :], -1)
        times = times + jnp.where(slot == named, 1, 0)
    present = jnp.where(times > 0, 1.0, 0.0)
    inner = jnp.where(iota((blocks, blocks), 0) < iota((blocks, blocks), 1), 1.0, 0.0)
    rank = jnp.dot(present.astype(BF), inner.astype(BF), preferred_element_type=F32)
    rank = jnp.where(times > 0, rank, -2.0)
    number = jnp.dot(
        present.astype(BF), jnp.ones((blocks, LANES), BF), preferred_element_type=F32
    ).astype(I32)
    pairs = (number + 1) >> 1
    outer = jnp.where(iota((slots, slots), 1) <= iota((slots, slots), 0), 1.0, 0.0).astype(BF)
    ends = jnp.dot(outer, pairs.astype(F32).astype(BF), preferred_element_type=F32).astype(I32)
    used = jnp.where(number > 0, 1.0, 0.0).astype(BF)
    tally = jnp.dot(outer, used, preferred_element_type=F32).astype(I32)
    lane = iota((1, LANES), 1)

    def first_after(done):
        return jnp.sum(jnp.where(tally <= done, 1, 0), axis=0, keepdims=True)

    begin = jnp.zeros((1, LANES), I32)
    behind = jnp.zeros((1, LANES), I32)
    for part, last in ((0, near), (1, slots)):
        stop = ends[last - 1 : last, :]
        opening = first_after(behind)
        for chunk in range(chunks):
            spot = begin + lane + chunk * LANES
            past = ends <= spot
            source = jnp.sum(jnp.where(past, 1, 0), axis=0, keepdims=True)
            start = jnp.max(jnp.where(past, ends, 0), axis=0, keepdims=True)
            word = jnp.where(spot < stop, source + (spot - start) * 65536, opening + half * 65536)
            row = part * chunks + chunk
            plan[row : row + 1, :] = word
        row = rows - 3 + part
        plan[row : row + 1, :] = (stop - begin + (UNROLL - 1)) >> (UNROLL.bit_length() - 1)
        if part == 0:
            begin = stop
            behind = tally[last - 1 : last, :]
    live = tally[slots - 1 : slots, :]
    for chunk in range(users):
        spot = behind + lane + chunk * LANES
        row = 2 * chunks + chunk
        plan[row : row + 1, :] = jnp.where(spot < live, first_after(spot), first_after(behind))
    plan[rows - 1 : rows, :] = (live - behind + (BUILD - 1)) >> (BUILD.bit_length() - 1)
    limit = jnp.max(pairs)
    for group in range(slots // LANES):
        at = slice(group * LANES, (group + 1) * LANES)
        wide = [
            jnp.concatenate([value, jnp.zeros((LANES, LANES - blocks), F32)], axis=1).T[:blocks]
            for value in (rank[at], times[at].astype(F32))
        ]
        position = wide[0].astype(I32)
        entry = iota((blocks, LANES), 0) + wide[1].astype(I32) * 256
        entry = jnp.where((position & 1) == 1, entry * 65536, entry)
        position = position >> 1
        first = group * (half + 8)
        ranked[first + half : first + half + 8, :] = jnp.zeros((8, LANES), I32)

        def fill(t, carry):
            found = jnp.sum(jnp.where(position == t, entry, 0), axis=0, keepdims=True)
            ranked[pl.ds(first + t, 1), :] = found
            return carry

        lax.fori_loop(0, limit, fill, 0)
    sent.wait()


def target_features(blocks, positions, blade, hub, azimuth, feats, centre, tables, stage):
    middle = [
        jnp.sum(positions[axis * blocks : (axis + 1) * blocks, :], axis=(0, 1), keepdims=True)
        / (blocks * LANES)
        for axis in range(3)
    ]
    for axis in range(3):
        centre[axis : axis + 1, :] = jnp.broadcast_to(middle[axis], (1, LANES))
    ones = jnp.ones((8, LANES), F32)
    pad = jnp.zeros((FEATURES - 24, LANES), F32)
    for group in range(blocks // 8):
        first = group * 8
        at = [
            positions[axis * blocks + first : axis * blocks + first + 8, :] - middle[axis]
            for axis in range(3)
        ]
        norm = split3(at[0] * at[0] + at[1] * at[1] + at[2] * at[2] + core_square)
        parts = [split3(-2.0 * value) for value in at]
        rows = []
        for piece in (0, 1, 2, 0, 1, 0):
            rows += [parts[axis][piece] for axis in range(3)]
        rows += [ones, ones, ones, norm[0], norm[1], norm[2]]
        base = (group % 2) * 24 * 8
        for f, value in enumerate(rows):
            stage[base + f * 8 : base + f * 8 + 8, :] = value
        for t in range(8):
            picked = stage[pl.ds(base + t, 24, stride=8), :]
            feats[first + t] = jnp.concatenate([picked, pad], axis=0).astype(BF)
    lane = iota((8, LANES), 1)
    angle = jnp.zeros((8, LANES), F32)
    hubs = [jnp.zeros((8, LANES), F32) for _ in range(3)]
    for q in range(ROTORS * BLADES):
        turn = F32(2.0 * math.pi) * F32(q % BLADES) / F32(BLADES)
        angle = jnp.where(lane == q, azimuth[q // BLADES] + turn, angle)
        for axis in range(3):
            hubs[axis] = jnp.where(lane == q, hub[axis, q // BLADES], hubs[axis])
    sources = [jnp.cos(angle), jnp.sin(angle)] + hubs
    for group in range(blocks // 8):
        index = blade[group * 8 : group * 8 + 8, :]
        for n, source in enumerate(sources):
            tables[n, group * 8 : group * 8 + 8, :] = jnp.take_along_axis(source, index, axis=1)


def answer_kernel(blocks, boxes, rcap, asked, positions, strengths, _, message, packed, sems):
    quarter = boxes // 4
    sent = []
    for part in range(4):
        first = part * quarter

        def one(p, carry):
            for i in range(rcap):
                block = jnp.maximum(asked[p, i], 0)
                packed[p, pl.ds(i, 3, stride=rcap), :] = positions[pl.ds(block, 3, stride=blocks), :]
                packed[p, pl.ds(3 * rcap + i, 3, stride=rcap), :] = strengths[
                    pl.ds(block, 3, stride=blocks), :
                ]
            return carry

        lax.fori_loop(first, first + quarter, one, 0)
        peers = pl.ds(first, quarter)
        copy = pltpu.make_async_copy(
            packed.at[peers], message.at[peers, pl.ds(0, 6 * rcap), :], sems.at[part]
        )
        copy.start()
        sent.append(copy)
    for copy in sent:
        copy.wait()


def prepare(source, centre, rcap, stage, table_stage, o):
    ones = jnp.ones((8, LANES), F32)
    zeros = jnp.zeros((8, LANES), F32)
    at = [source(axis) - centre[axis : axis + 1, :] for axis in range(3)]
    gamma = [source(3 + axis) for axis in range(3)]
    parts = [split3(value) for value in at]
    norm = split3(at[0] * at[0] + at[1] * at[1] + at[2] * at[2])
    values = []
    for piece in (0, 0, 0, 1, 1, 2):
        values += [parts[axis][piece] for axis in range(3)]
    values += [norm[0], norm[1], norm[2], ones, ones, ones]
    for f, value in enumerate(values):
        stage[o, f * 8 : f * 8 + 8, :] = value
    for axis in range(3):
        left, right = (axis + 1) % 3, (axis + 2) % 3
        table_stage[o, axis * 8 : axis * 8 + 8, :] = gamma[axis]
        table_stage[o, (3 + axis) * 8 : (4 + axis) * 8, :] = (
            at[left] * gamma[right] - at[right] * gamma[left]
        )
    table_stage[o, 48:56, :] = zeros
    table_stage[o, 56:64, :] = zeros


def build(slot, identity, stage, table_stage, feats, tables):
    zeros = jnp.zeros((8, LANES), F32)
    pad = jnp.zeros((LANES - 24, LANES), F32)
    o = slot >> 3
    i = slot & 7
    picked = jnp.concatenate([stage[o, pl.ds(i, 24, stride=8), :], pad], axis=0)
    turned = lax.dot_general(
        identity, picked.astype(BF), (((1,), (1,)), ((), ())), preferred_element_type=F32
    )
    feats[slot] = turned.astype(BF)
    table = table_stage[o, pl.ds(i, 8, stride=8), :]
    high = table.astype(BF).astype(F32)
    left = jnp.concatenate([high, table - high], axis=0)
    right = jnp.concatenate([high, zeros], axis=0)
    tables[slot] = jnp.concatenate([left, right], axis=1).astype(BF)


def unit():
    return jnp.where(iota((LANES, LANES), 0) == iota((LANES, LANES), 1), 1.0, 0.0).astype(BF)


def gather_pairs(first, number, slots, half, plan, ranked, targets, feats, tables, sums0, sums1, held):
    held[...] = jnp.zeros_like(held)
    empty = jnp.zeros((LANES - FEATURES, 2 * LANES), BF)

    def named(it):
        found = []
        for u in range(UNROLL):
            at = it * UNROLL + u
            word = plan[first + (at >> 7), at & 127]
            slot = word & 65535
            row = word >> 16
            if slots > LANES:
                row = row + (slot >> 7) * (half + 8)
            found.append((slot, ranked[row, slot & 127]))
        return found

    def flush(it):
        for u, (_, pair) in enumerate(named(it)):
            for sums, word, part in (
                (sums0, pair & 65535, held[u, :, :LANES]),
                (sums1, pair >> 16, held[u, :, LANES:]),
            ):
                at = pl.ds(pl.multiple_of((word & 255) * 8, 8), 8)
                sums[at, :] = sums[at, :] + (word >> 8).astype(F32) * part

    def accumulate(it, carry):
        flush(jnp.maximum(it - 1, 0))
        for u, (slot, pair) in enumerate(named(it)):
            both = jnp.concatenate([targets[pair & 255], targets[(pair >> 16) & 255]], axis=1)
            both = jnp.concatenate([both, empty], axis=0)
            inverse = lax.rsqrt(jnp.dot(feats[slot], both, preferred_element_type=F32))
            weight = inverse * inverse * inverse
            high = weight.astype(BF)
            low = (weight - high.astype(F32)).astype(BF)
            summed = jnp.dot(
                tables[slot], jnp.concatenate([high, low], axis=0), preferred_element_type=F32
            )
            held[u] = summed[:8] + summed[8:]
        return carry

    lax.fori_loop(0, number, accumulate, 0)

    @pl.when(number > 0)
    def _():
        flush(number - 1)


def near_kernel(blocks, boxes, rcap, cap, slots, half, most, plan, ranked, asked, labels, hub,
                azimuth, places, gammas, mate_places, mate_gammas, blade,
                partial, targets, centre, turns, moved_from, aged_from,
                target_stage, local, stage, table_stage, feats, tables, sums0, sums1, held):
    target_features(blocks, places, blade, hub, azimuth, targets, centre, turns, target_stage)

    def peer(p, carry):
        for target, lane, number in ((moved_from, rcap, 0), (aged_from, rcap + cap, 1)):

            def label(rank, carry):
                target[labels[p, lane + rank]] = p * 256 + rank
                return carry

            lax.fori_loop(0, labels[p, rcap + 2 * cap + number], label, 0)
        return carry

    lax.fori_loop(0, boxes, peer, 0)
    _, _, rows = plan_rows(slots, most)
    me = lax.axis_index("box")
    for o, (from_places, from_gammas) in enumerate(((places, gammas), (mate_places, mate_gammas))):
        for i in range(rcap):
            block = jnp.maximum(asked[i, me ^ o], 0)
            local[o, pl.ds(i, 3, stride=rcap), :] = from_places[pl.ds(block, 3, stride=blocks), :]
            local[o, pl.ds(3 * rcap + i, 3, stride=rcap), :] = from_gammas[
                pl.ds(block, 3, stride=blocks), :
            ]
    for o in range(2):
        prepare(
            lambda c: local[o, c * rcap : (c + 1) * rcap, :], centre, rcap, stage, table_stage, o
        )
    identity = unit()
    for slot in range(2 * rcap):
        build(slot, identity, stage, table_stage, feats, tables)
    sums0[...] = jnp.zeros_like(sums0)
    sums1[...] = jnp.zeros_like(sums1)
    gather_pairs(
        0, plan[rows - 3, 0], slots, half, plan, ranked, targets, feats, tables, sums0, sums1, held
    )
    partial[...] = sums0[...] + sums1[...]


def far_kernel(blocks, boxes, rcap, cap, slots, half, most, plan, ranked, moved_from, age_place,
               fetched, positions, targets, centre, partial,
               new_positions, new_history, outgoing,
               speed, stage, table_stage, feats, tables, sums0, sums1, held):
    chunks, _, rows = plan_rows(slots, most)
    me = lax.axis_index("box")

    def owner(o, carry):
        at = o ^ me
        prepare(
            lambda c: fetched[at, c * rcap : (c + 1) * rcap, :], centre, rcap, stage, table_stage, o
        )
        return carry

    lax.fori_loop(2, boxes, owner, 0, unroll=2)
    identity = unit()

    def several(it, carry):
        for u in range(BUILD):
            at = it * BUILD + u
            slot = plan[2 * chunks + (at >> 7), at & 127]
            build(slot, identity, stage, table_stage, feats, tables)
        return carry

    lax.fori_loop(0, plan[rows - 1, 0], several, 0)
    sums0[...] = partial[...]
    sums1[...] = jnp.zeros_like(sums1)
    gather_pairs(
        chunks, plan[rows - 2, 0], slots, half, plan, ranked, targets, feats, tables,
        sums0, sums1, held,
    )
    scale = 1.0 / (4.0 * math.pi)
    for group in range(blocks // 8):
        first = group * 8
        total = [
            sums0[pl.ds(first * 8 + f, 8, stride=8), :] + sums1[pl.ds(first * 8 + f, 8, stride=8), :]
            for f in range(6)
        ]
        at = [
            positions[axis * blocks + first : axis * blocks + first + 8, :]
            - centre[axis : axis + 1, :]
            for axis in range(3)
        ]
        for axis in range(3):
            left, right = (axis + 1) % 3, (axis + 2) % 3
            speed[axis * blocks + first : axis * blocks + first + 8, :] = scale * (
                at[left] * total[right] - at[right] * total[left] - total[3 + axis]
            )
    unused = jnp.zeros((3 * cap, LANES), F32)

    def clear(p, carry):
        outgoing[p] = unused
        return carry

    lax.fori_loop(0, boxes, clear, 0)

    def finish(b, carry):
        where = moved_from[b]
        box = where >> 8
        rank = where & 255
        recent = fetched[box, pl.ds(6 * rcap + rank, 3, stride=cap), :]
        older = fetched[box, pl.ds(6 * rcap + 3 * cap + rank, 3, stride=cap), :]
        rows = pl.ds(b, 3, stride=blocks)
        now = speed[rows, :]
        stepped = positions[rows, :] + time_step * (23.0 * now - 16.0 * recent + 5.0 * older) / 12.0
        new_positions[rows, :] = stepped
        for axis in range(3):
            new_history[b, axis, 0:1, :] = now[axis : axis + 1]
            new_history[b, axis, 1:2, :] = recent[axis : axis + 1]
        out = age_place[b]
        outgoing[out >> 8, pl.ds(out & 255, 3, stride=cap), :] = stepped
        return carry

    lax.fori_loop(0, blocks, finish, 0, unroll=4)


def frame_kernel(blocks, cap, aged_from, arrived, tables, frame):
    def one(b, carry):
        where = aged_from[b]
        aged = arrived[where >> 8, pl.ds(where & 255, 3, stride=cap), :]
        cosine, sine, hub0, hub1, hub2 = [tables[n, pl.ds(b, 1), :] for n in range(5)]
        first = aged[0:1] - hub0
        second = aged[1:2] - hub1
        frame[pl.ds(b, 1), :] = cosine * first + sine * second
        frame[pl.ds(blocks + b, 1), :] = cosine * second - sine * first
        frame[pl.ds(2 * blocks + b, 1), :] = aged[2:3] - hub2
        return carry

    lax.fori_loop(0, blocks, one, 0, unroll=8)


def swap(values):
    return lax.all_to_all(values, "box", split_axis=0, concat_axis=0, tiled=True)


def call(kernel, name, in_specs, outs, scratch=(), aliases={}):
    several = isinstance(outs, list)
    listed = outs if several else [outs]
    specs = [spec for spec, _, _ in listed]
    shapes = [jax.ShapeDtypeStruct(dims, dtype) for _, dims, dtype in listed]
    return pl.pallas_call(
        kernel,
        in_specs=in_specs,
        out_specs=specs if several else specs[0],
        out_shape=shapes if several else shapes[0],
        scratch_shapes=list(scratch),
        input_output_aliases=aliases,
        compiler_params=pltpu.CompilerParams(vmem_limit_bytes=60 << 20),
        name=name,
    )


def body(
    positions,
    strengths,
    history,
    move_list,
    age_slot,
    fetch_list,
    tile_slot,
    tile_count,
    blade_id,
    hub_centre,
    azimuth,
):
    blocks = positions.shape[0]
    boxes = lax.axis_size("box")
    rcap = fetch_list.shape[2]
    kmax = tile_slot.shape[1]
    cap = 2 * blocks // boxes
    slots = boxes * rcap
    most = (blocks * kmax + slots) // 2 + UNROLL
    chunks, users, rows = plan_rows(slots, most)
    groups = slots // LANES

    places = jnp.transpose(positions, (1, 0, 2)).reshape(3 * blocks, LANES)
    gammas = jnp.transpose(strengths, (1, 0, 2)).reshape(3 * blocks, LANES)
    past = jnp.transpose(history, (0, 2, 1, 3))

    asked = fetch_list[0].T
    meta, move_place, age_place = call(
        functools.partial(meta_kernel, blocks, boxes, rcap, cap),
        "meta",
        [SMEM] * 3,
        [(SMEM, (boxes, LANES), I32), (SMEM, (blocks,), I32), (SMEM, (blocks,), I32)],
        [pltpu.SMEM((2 * boxes,), I32)],
    )(move_list, age_slot, asked)
    labels = swap(meta)
    past_rows = (6 * cap + 7) // 8 * 8
    message_shape = (boxes, 6 * rcap + past_rows, LANES)
    message, plan, ranked = call(
        functools.partial(plan_kernel, blocks, kmax, rcap, cap, slots, most),
        "plan",
        [SMEM] + [VMEM] * 3,
        [
            (ANY, message_shape, F32),
            (VMEM, (rows, LANES), I32),
            (VMEM, (groups * (kmax + 8), LANES), I32),
        ],
        [pltpu.VMEM((boxes, past_rows, LANES), F32), pltpu.SemaphoreType.DMA],
    )(move_place, past, tile_slot.T, tile_count.reshape(1, blocks))
    mates = [(box, box ^ 1) for box in range(boxes)]
    mate_places = lax.ppermute(places, "box", mates)
    mate_gammas = lax.ppermute(gammas, "box", mates)
    labels, message, plan, ranked, mate_places, mate_gammas = lax.optimization_barrier(
        (labels, message, plan, ranked, mate_places, mate_gammas)
    )
    message = call(
        functools.partial(answer_kernel, blocks, boxes, rcap),
        "answer",
        [SMEM, VMEM, VMEM, ANY],
        (ANY, message_shape, F32),
        [pltpu.VMEM((boxes, 6 * rcap, LANES), F32), pltpu.SemaphoreType.DMA((4,))],
        {3: 0},
    )(labels, places, gammas, message)
    plan, ranked, mate_places, message = lax.optimization_barrier(
        (plan, ranked, mate_places, message)
    )
    fetched = swap(message)

    def scratch(owners):
        return [
            pltpu.VMEM((owners, 24 * 8, LANES), F32),
            pltpu.VMEM((owners, 64, LANES), F32),
            pltpu.VMEM((owners * rcap, LANES, LANES), BF),
            pltpu.VMEM((owners * rcap, 16, 2 * LANES), BF),
            pltpu.VMEM((blocks * 8, LANES), F32),
            pltpu.VMEM((blocks * 8, LANES), F32),
            pltpu.VMEM((UNROLL, 8, 2 * LANES), F32),
        ]

    partial, targets, centre, turns, moved_from, aged_from = call(
        functools.partial(near_kernel, blocks, boxes, rcap, cap, slots, kmax, most),
        "near",
        [SMEM] * 6 + [VMEM] * 5,
        [
            (VMEM, (blocks * 8, LANES), F32),
            (VMEM, (blocks, FEATURES, LANES), BF),
            (VMEM, (8, LANES), F32),
            (VMEM, (5, blocks, LANES), F32),
            (SMEM, (blocks,), I32),
            (SMEM, (blocks,), I32),
        ],
        [pltpu.VMEM((2 * 24 * 8, LANES), F32), pltpu.VMEM((2, 6 * rcap, LANES), F32)] + scratch(2),
    )(
        plan, ranked, asked, labels, hub_centre.T, azimuth,
        places, gammas, mate_places, mate_gammas, blade_id,
    )
    fetched, partial = lax.optimization_barrier((fetched, partial))
    new_positions, new_history, outgoing = call(
        functools.partial(far_kernel, blocks, boxes, rcap, cap, slots, kmax, most),
        "far",
        [SMEM] * 4 + [VMEM] * 5,
        [
            (VMEM, (3 * blocks, LANES), F32),
            (VMEM, (blocks, 3, 2, LANES), F32),
            (VMEM, (boxes, 3 * cap, LANES), F32),
        ],
        [pltpu.VMEM((3 * blocks, LANES), F32)] + scratch(boxes),
    )(plan, ranked, moved_from, age_place, fetched, places, targets, centre, partial)
    aged = swap(outgoing)
    frame = call(
        functools.partial(frame_kernel, blocks, cap),
        "frame",
        [SMEM, VMEM, VMEM],
        (VMEM, (3 * blocks, LANES), F32),
    )(aged_from, aged, turns)

    def back(rows):
        return jnp.transpose(rows.reshape(3, blocks, LANES), (1, 0, 2))

    return back(new_positions), jnp.transpose(new_history, (0, 2, 1, 3)), back(frame)


def solution(mesh):
    split = ("cases", "box")
    placed = (
        P(split, None, None),
        P(split, None, None),
        P(split, None, None, None),
        P(split),
        P(split),
        P(split, None, None),
        P(split, None),
        P(split),
        P(split, None),
        P("cases", None),
        P("cases"),
    )
    return jax.shard_map(
        body,
        mesh=mesh,
        in_specs=placed,
        out_specs=(P(split, None, None), P(split, None, None, None), P(split, None, None)),
        check_vma=False,
    )
```

```python
import functools
import math

import jax
import jax.numpy as jnp
from jax import lax
from jax.experimental import pallas as pl
from jax.experimental.pallas import tpu as pltpu
from jax.sharding import PartitionSpec as P

ROTORS = 6
BLADES = 3

core_square = 0.05
time_step = 0.05

LANES = 128
FEATURES = 32
UNROLL = 48
BUILD = 8
BF = jnp.bfloat16
F32 = jnp.float32
I32 = jnp.int32

SMEM = pl.BlockSpec(memory_space=pltpu.SMEM)
VMEM = pl.BlockSpec(memory_space=pltpu.VMEM)
ANY = pl.BlockSpec(memory_space=pl.ANY)


def split3(value):
    high = value.astype(BF).astype(F32)
    rest = value - high
    middle = rest.astype(BF).astype(F32)
    return high, middle, rest - middle


def iota(dims, axis):
    return lax.broadcasted_iota(I32, dims, axis)


def meta_kernel(blocks, boxes, rcap, cap, move, age, fetch, meta):
    def product(left, right, contract=1):
        return lax.dot_general(
            left.astype(BF), right.astype(BF), (((1,), (contract,)), ((), ())),
            preferred_element_type=F32,
        )

    def flag(condition):
        return jnp.where(condition, 1.0, 0.0)

    asked = product(flag(iota((boxes, boxes), 0) == iota((boxes, boxes), 1)), fetch[...].astype(F32), 1)
    row = product(asked, flag(iota((rcap, LANES), 0) == iota((rcap, LANES), 1)), 0)
    before = flag(iota((blocks, blocks), 0) < iota((blocks, blocks), 1))
    diagonal = iota((blocks, blocks), 0) == iota((blocks, blocks), 1)
    lane = iota((blocks, LANES), 1)
    for n, source in enumerate((move, age)):
        block = source[...]
        sent = flag(lax.div(block, blocks) == iota((boxes, blocks), 0))
        rank = jnp.sum(sent * product(sent, before, 0), axis=0, keepdims=True)
        turned = product(jnp.where(diagonal, rank, 0.0), jnp.ones((blocks, LANES), F32), 0)
        place = flag(turned.astype(I32) + (rcap + n * cap) == lane)
        row = row + product(sent * lax.rem(block, blocks).astype(F32), place, 0)
        row = row + product(sent, flag(lane == rcap + 2 * cap + n), 0)
    meta[...] = row.astype(I32)


def plan_rows(slots, most):
    chunks = (most + LANES - 1) // LANES
    users = (slots + BUILD + LANES - 1) // LANES
    return chunks, users, (2 * chunks + users + 3 + 7) // 8 * 8


def plan_kernel(blocks, boxes, kmax, rcap, cap, slots, most, move, age, history, tiles, count,
                message, plan, ranked, age_place, packed, filled, sem):
    def clear(p, carry):
        filled[p] = 0
        return carry

    lax.fori_loop(0, 2 * boxes, clear, 0, unroll=8)
    shift = blocks.bit_length() - 1

    def owner(block):
        return block >> shift if 1 << shift == blocks else lax.div(block, blocks)

    def one(g, carry):
        box = owner(age[g])
        rank = filled[boxes + box]
        filled[boxes + box] = rank + 1
        age_place[g] = box * 256 + rank
        box = owner(move[g])
        rank = filled[box]
        filled[box] = rank + 1
        for axis in range(3):
            packed[box, pl.ds(axis * cap + rank, 2, stride=3 * cap), :] = history[g, axis]
        return carry

    lax.fori_loop(0, blocks, one, 0, unroll=8)
    sent = pltpu.make_async_copy(packed, message.at[:, pl.ds(6 * rcap, packed.shape[1]), :], sem)
    sent.start()
    half = kmax
    near = 2 * rcap
    chunks, users, rows = plan_rows(slots, most)
    turn = lax.axis_index("box") * rcap
    slot = iota((slots, blocks), 0) ^ turn
    times = jnp.zeros((slots, blocks), I32)
    for k in range(kmax):
        named = jnp.where(count[...] > k, tiles[k : k + 1, :], -1)
        times = times + jnp.where(slot == named, 1, 0)
    present = jnp.where(times > 0, 1.0, 0.0)
    inner = jnp.where(iota((blocks, blocks), 0) < iota((blocks, blocks), 1), 1.0, 0.0)
    rank = jnp.dot(present.astype(BF), inner.astype(BF), preferred_element_type=F32)
    rank = jnp.where(times > 0, rank, -2.0)
    number = jnp.dot(
        present.astype(BF), jnp.ones((blocks, LANES), BF), preferred_element_type=F32
    ).astype(I32)
    pairs = (number + 1) >> 1
    outer = jnp.where(iota((slots, slots), 1) <= iota((slots, slots), 0), 1.0, 0.0).astype(BF)
    ends = jnp.dot(outer, pairs.astype(F32).astype(BF), preferred_element_type=F32).astype(I32)
    used = jnp.where(number > 0, 1.0, 0.0).astype(BF)
    tally = jnp.dot(outer, used, preferred_element_type=F32).astype(I32)
    lane = iota((1, LANES), 1)

    def first_after(done):
        return jnp.sum(jnp.where(tally <= done, 1, 0), axis=0, keepdims=True)

    begin = jnp.zeros((1, LANES), I32)
    behind = jnp.zeros((1, LANES), I32)
    for part, last in ((0, near), (1, slots)):
        stop = ends[last - 1 : last, :]
        opening = first_after(behind)
        for chunk in range(chunks):
            spot = begin + lane + chunk * LANES
            past = ends <= spot
            source = jnp.sum(jnp.where(past, 1, 0), axis=0, keepdims=True)
            start = jnp.max(jnp.where(past, ends, 0), axis=0, keepdims=True)
            word = jnp.where(spot < stop, source + (spot - start) * 65536, opening + half * 65536)
            row = part * chunks + chunk
            plan[row : row + 1, :] = word
        row = rows - 3 + part
        plan[row : row + 1, :] = lax.div(stop - begin + (UNROLL - 1), UNROLL)
        if part == 0:
            begin = stop
            behind = tally[last - 1 : last, :]
    live = tally[slots - 1 : slots, :]
    for chunk in range(users):
        spot = behind + lane + chunk * LANES
        row = 2 * chunks + chunk
        plan[row : row + 1, :] = jnp.where(spot < live, first_after(spot), first_after(behind))
    plan[rows - 1 : rows, :] = (live - behind + (BUILD - 1)) >> (BUILD.bit_length() - 1)
    limit = jnp.max(pairs)
    for group in range(slots // LANES):
        at = slice(group * LANES, (group + 1) * LANES)
        wide = [
            jnp.concatenate([value, jnp.zeros((LANES, LANES - blocks), F32)], axis=1).T[:blocks]
            for value in (rank[at], times[at].astype(F32))
        ]
        position = wide[0].astype(I32)
        entry = iota((blocks, LANES), 0) + wide[1].astype(I32) * 256
        entry = jnp.where((position & 1) == 1, entry * 65536, entry)
        position = position >> 1
        first = group * (half + 8)
        ranked[first + half : first + half + 8, :] = jnp.zeros((8, LANES), I32)

        def fill(t, carry):
            found = jnp.sum(jnp.where(position == t, entry, 0), axis=0, keepdims=True)
            ranked[pl.ds(first + t, 1), :] = found
            return carry

        lax.fori_loop(0, limit, fill, 0)
    sent.wait()


def target_features(blocks, positions, blade, hub, azimuth, feats, centre, tables, stage):
    middle = [
        jnp.sum(positions[axis * blocks : (axis + 1) * blocks, :], axis=(0, 1), keepdims=True)
        / (blocks * LANES)
        for axis in range(3)
    ]
    for axis in range(3):
        centre[axis : axis + 1, :] = jnp.broadcast_to(middle[axis], (1, LANES))
    ones = jnp.ones((8, LANES), F32)
    pad = jnp.zeros((FEATURES - 24, LANES), F32)
    for group in range(blocks // 8):
        first = group * 8
        at = [
            positions[axis * blocks + first : axis * blocks + first + 8, :] - middle[axis]
            for axis in range(3)
        ]
        norm = split3(at[0] * at[0] + at[1] * at[1] + at[2] * at[2] + core_square)
        parts = [split3(-2.0 * value) for value in at]
        rows = []
        for piece in (0, 1, 2, 0, 1, 0):
            rows += [parts[axis][piece] for axis in range(3)]
        rows += [ones, ones, ones, norm[0], norm[1], norm[2]]
        base = (group % 2) * 24 * 8
        for f, value in enumerate(rows):
            stage[base + f * 8 : base + f * 8 + 8, :] = value
        for t in range(8):
            picked = stage[pl.ds(base + t, 24, stride=8), :]
            feats[first + t] = jnp.concatenate([picked, pad], axis=0).astype(BF)
    lane = iota((8, LANES), 1)
    angle = jnp.zeros((8, LANES), F32)
    hubs = [jnp.zeros((8, LANES), F32) for _ in range(3)]
    for q in range(ROTORS * BLADES):
        turn = F32(2.0 * math.pi) * F32(q % BLADES) / F32(BLADES)
        angle = jnp.where(lane == q, azimuth[q // BLADES] + turn, angle)
        for axis in range(3):
            hubs[axis] = jnp.where(lane == q, hub[axis, q // BLADES], hubs[axis])
    sources = [jnp.cos(angle), jnp.sin(angle)] + hubs
    for group in range(blocks // 8):
        index = blade[group * 8 : group * 8 + 8, :]
        for n, source in enumerate(sources):
            tables[n, group * 8 : group * 8 + 8, :] = jnp.take_along_axis(source, index, axis=1)


def answer_kernel(blocks, boxes, rcap, asked, positions, strengths, _, message, packed, sems):
    quarter = boxes // 4
    sent = []
    for part in range(4):
        first = part * quarter

        def one(p, carry):
            for i in range(rcap):
                block = jnp.maximum(asked[p, i], 0)
                packed[p, pl.ds(i, 3, stride=rcap), :] = positions[pl.ds(block, 3, stride=blocks), :]
                packed[p, pl.ds(3 * rcap + i, 3, stride=rcap), :] = strengths[
                    pl.ds(block, 3, stride=blocks), :
                ]
            return carry

        lax.fori_loop(first, first + quarter, one, 0)
        peers = pl.ds(first, quarter)
        copy = pltpu.make_async_copy(
            packed.at[peers], message.at[peers, pl.ds(0, 6 * rcap), :], sems.at[part]
        )
        copy.start()
        sent.append(copy)
    for copy in sent:
        copy.wait()


def prepare(source, centre, rcap, stage, table_stage, o):
    ones = jnp.ones((8, LANES), F32)
    zeros = jnp.zeros((8, LANES), F32)
    at = [source(axis) - centre[axis : axis + 1, :] for axis in range(3)]
    gamma = [source(3 + axis) for axis in range(3)]
    parts = [split3(value) for value in at]
    norm = split3(at[0] * at[0] + at[1] * at[1] + at[2] * at[2])
    values = []
    for piece in (0, 0, 0, 1, 1, 2):
        values += [parts[axis][piece] for axis in range(3)]
    values += [norm[0], norm[1], norm[2], ones, ones, ones]
    for f, value in enumerate(values):
        stage[o, f * 8 : f * 8 + 8, :] = value
    for axis in range(3):
        left, right = (axis + 1) % 3, (axis + 2) % 3
        table_stage[o, axis * 8 : axis * 8 + 8, :] = gamma[axis]
        table_stage[o, (3 + axis) * 8 : (4 + axis) * 8, :] = (
            at[left] * gamma[right] - at[right] * gamma[left]
        )
    table_stage[o, 48:56, :] = zeros
    table_stage[o, 56:64, :] = zeros


def build(slot, identity, stage, table_stage, feats, tables):
    zeros = jnp.zeros((8, LANES), F32)
    pad = jnp.zeros((LANES - 24, LANES), F32)
    o = slot >> 3
    i = slot & 7
    picked = jnp.concatenate([stage[o, pl.ds(i, 24, stride=8), :], pad], axis=0)
    turned = lax.dot_general(
        identity, picked.astype(BF), (((1,), (1,)), ((), ())), preferred_element_type=F32
    )
    feats[slot] = turned.astype(BF)
    table = table_stage[o, pl.ds(i, 8, stride=8), :]
    high = table.astype(BF).astype(F32)
    left = jnp.concatenate([high, table - high], axis=0)
    right = jnp.concatenate([high, zeros], axis=0)
    tables[slot] = jnp.concatenate([left, right], axis=1).astype(BF)


def unit():
    return jnp.where(iota((LANES, LANES), 0) == iota((LANES, LANES), 1), 1.0, 0.0).astype(BF)


def gather_pairs(first, number, slots, half, plan, ranked, targets, feats, tables, sums0, sums1, held):
    held[...] = jnp.zeros_like(held)
    empty = jnp.zeros((LANES - FEATURES, 2 * LANES), BF)

    def named(it):
        found = []
        for u in range(UNROLL):
            at = it * UNROLL + u
            word = plan[first + (at >> 7), at & 127]
            slot = word & 65535
            row = word >> 16
            if slots > LANES:
                row = row + (slot >> 7) * (half + 8)
            found.append((slot, ranked[row, slot & 127]))
        return found

    def flush(it):
        for u, (_, pair) in enumerate(named(it)):
            for sums, word, part in (
                (sums0, pair & 65535, held[u, :, :LANES]),
                (sums1, pair >> 16, held[u, :, LANES:]),
            ):
                at = pl.ds(pl.multiple_of((word & 255) * 8, 8), 8)
                sums[at, :] = sums[at, :] + (word >> 8).astype(F32) * part

    def accumulate(it, carry):
        flush(jnp.maximum(it - 1, 0))
        for u, (slot, pair) in enumerate(named(it)):
            both = jnp.concatenate([targets[pair & 255], targets[(pair >> 16) & 255]], axis=1)
            both = jnp.concatenate([both, empty], axis=0)
            inverse = lax.rsqrt(jnp.dot(feats[slot], both, preferred_element_type=F32))
            weight = inverse * inverse * inverse
            high = weight.astype(BF)
            low = (weight - high.astype(F32)).astype(BF)
            summed = jnp.dot(
                tables[slot], jnp.concatenate([high, low], axis=0), preferred_element_type=F32
            )
            held[u] = summed[:8] + summed[8:]
        return carry

    lax.fori_loop(0, number, accumulate, 0)

    @pl.when(number > 0)
    def _():
        flush(number - 1)


def near_kernel(blocks, boxes, rcap, cap, slots, half, most, plan, ranked, asked, labels, hub,
                azimuth, places, gammas, mate_places, mate_gammas, blade,
                partial, targets, centre, turns, moved_from, aged_from,
                target_stage, local, stage, table_stage, feats, tables, sums0, sums1, held):
    target_features(blocks, places, blade, hub, azimuth, targets, centre, turns, target_stage)

    def peer(p, carry):
        for target, lane, number in ((moved_from, rcap, 0), (aged_from, rcap + cap, 1)):

            def label(rank, carry):
                target[labels[p, lane + rank]] = p * 256 + rank
                return carry

            lax.fori_loop(0, labels[p, rcap + 2 * cap + number], label, 0)
        return carry

    lax.fori_loop(0, boxes, peer, 0)
    _, _, rows = plan_rows(slots, most)
    me = lax.axis_index("box")
    for o, (from_places, from_gammas) in enumerate(((places, gammas), (mate_places, mate_gammas))):
        for i in range(rcap):
            block = jnp.maximum(asked[i, me ^ o], 0)
            local[o, pl.ds(i, 3, stride=rcap), :] = from_places[pl.ds(block, 3, stride=blocks), :]
            local[o, pl.ds(3 * rcap + i, 3, stride=rcap), :] = from_gammas[
                pl.ds(block, 3, stride=blocks), :
            ]
    for o in range(2):
        prepare(
            lambda c: local[o, c * rcap : (c + 1) * rcap, :], centre, rcap, stage, table_stage, o
        )
    identity = unit()
    for slot in range(2 * rcap):
        build(slot, identity, stage, table_stage, feats, tables)
    sums0[...] = jnp.zeros_like(sums0)
    sums1[...] = jnp.zeros_like(sums1)
    gather_pairs(
        0, plan[rows - 3, 0], slots, half, plan, ranked, targets, feats, tables, sums0, sums1, held
    )
    partial[...] = sums0[...] + sums1[...]


def far_kernel(blocks, boxes, rcap, cap, slots, half, most, plan, ranked, moved_from, age_place,
               fetched, positions, targets, centre, partial,
               new_positions, new_history, outgoing,
               speed, stage, table_stage, feats, tables, sums0, sums1, held):
    chunks, _, rows = plan_rows(slots, most)
    me = lax.axis_index("box")

    def owner(o, carry):
        at = o ^ me
        prepare(
            lambda c: fetched[at, c * rcap : (c + 1) * rcap, :], centre, rcap, stage, table_stage, o
        )
        return carry

    lax.fori_loop(2, boxes, owner, 0, unroll=2)
    identity = unit()

    def several(it, carry):
        for u in range(BUILD):
            at = it * BUILD + u
            slot = plan[2 * chunks + (at >> 7), at & 127]
            build(slot, identity, stage, table_stage, feats, tables)
        return carry

    lax.fori_loop(0, plan[rows - 1, 0], several, 0)
    sums0[...] = partial[...]
    sums1[...] = jnp.zeros_like(sums1)
    gather_pairs(
        chunks, plan[rows - 2, 0], slots, half, plan, ranked, targets, feats, tables,
        sums0, sums1, held,
    )
    scale = 1.0 / (4.0 * math.pi)
    for group in range(blocks // 8):
        first = group * 8
        total = [
            sums0[pl.ds(first * 8 + f, 8, stride=8), :] + sums1[pl.ds(first * 8 + f, 8, stride=8), :]
            for f in range(6)
        ]
        at = [
            positions[axis * blocks + first : axis * blocks + first + 8, :]
            - centre[axis : axis + 1, :]
            for axis in range(3)
        ]
        for axis in range(3):
            left, right = (axis + 1) % 3, (axis + 2) % 3
            speed[axis * blocks + first : axis * blocks + first + 8, :] = scale * (
                at[left] * total[right] - at[right] * total[left] - total[3 + axis]
            )
    unused = jnp.zeros((3 * cap, LANES), F32)

    def clear(p, carry):
        outgoing[p] = unused
        return carry

    lax.fori_loop(0, boxes, clear, 0)

    def finish(b, carry):
        where = moved_from[b]
        box = where >> 8
        rank = where & 255
        recent = fetched[box, pl.ds(6 * rcap + rank, 3, stride=cap), :]
        older = fetched[box, pl.ds(6 * rcap + 3 * cap + rank, 3, stride=cap), :]
        rows = pl.ds(b, 3, stride=blocks)
        now = speed[rows, :]
        stepped = positions[rows, :] + time_step * (23.0 * now - 16.0 * recent + 5.0 * older) / 12.0
        new_positions[rows, :] = stepped
        for axis in range(3):
            new_history[b, axis, 0:1, :] = now[axis : axis + 1]
            new_history[b, axis, 1:2, :] = recent[axis : axis + 1]
        out = age_place[b]
        outgoing[out >> 8, pl.ds(out & 255, 3, stride=cap), :] = stepped
        return carry

    lax.fori_loop(0, blocks, finish, 0, unroll=4)


def frame_kernel(blocks, cap, aged_from, arrived, tables, frame):
    def one(b, carry):
        where = aged_from[b]
        aged = arrived[where >> 8, pl.ds(where & 255, 3, stride=cap), :]
        cosine, sine, hub0, hub1, hub2 = [tables[n, pl.ds(b, 1), :] for n in range(5)]
        first = aged[0:1] - hub0
        second = aged[1:2] - hub1
        frame[pl.ds(b, 1), :] = cosine * first + sine * second
        frame[pl.ds(blocks + b, 1), :] = cosine * second - sine * first
        frame[pl.ds(2 * blocks + b, 1), :] = aged[2:3] - hub2
        return carry

    lax.fori_loop(0, blocks, one, 0, unroll=8)


def swap(values):
    return lax.all_to_all(values, "box", split_axis=0, concat_axis=0, tiled=True)


def call(kernel, name, in_specs, outs, scratch=(), aliases={}, limit=65400 << 10):
    several = isinstance(outs, list)
    listed = outs if several else [outs]
    specs = [spec for spec, _, _ in listed]
    shapes = [jax.ShapeDtypeStruct(dims, dtype) for _, dims, dtype in listed]
    return pl.pallas_call(
        kernel,
        in_specs=in_specs,
        out_specs=specs if several else specs[0],
        out_shape=shapes if several else shapes[0],
        scratch_shapes=list(scratch),
        input_output_aliases=aliases,
        compiler_params=pltpu.CompilerParams(vmem_limit_bytes=limit),
        name=name,
    )


def body(
    positions,
    strengths,
    history,
    move_list,
    age_slot,
    fetch_list,
    tile_slot,
    tile_count,
    blade_id,
    hub_centre,
    azimuth,
):
    blocks = positions.shape[0]
    boxes = lax.axis_size("box")
    rcap = fetch_list.shape[2]
    kmax = tile_slot.shape[1]
    cap = 2 * blocks // boxes
    slots = boxes * rcap
    most = (blocks * kmax + slots) // 2 + UNROLL
    chunks, users, rows = plan_rows(slots, most)
    groups = slots // LANES

    places = jnp.transpose(positions, (1, 0, 2)).reshape(3 * blocks, LANES)
    gammas = jnp.transpose(strengths, (1, 0, 2)).reshape(3 * blocks, LANES)
    past = jnp.transpose(history, (0, 2, 1, 3))

    asked = fetch_list[0].T
    meta = call(
        functools.partial(meta_kernel, blocks, boxes, rcap, cap),
        "meta",
        [VMEM] * 3,
        (VMEM, (boxes, LANES), I32),
    )(move_list.reshape(1, blocks), age_slot.reshape(1, blocks), asked)
    labels = swap(meta)
    past_rows = (6 * cap + 7) // 8 * 8
    message_shape = (boxes, 6 * rcap + past_rows, LANES)
    message, plan, ranked, age_place = call(
        functools.partial(plan_kernel, blocks, boxes, kmax, rcap, cap, slots, most),
        "plan",
        [SMEM] * 2 + [VMEM] * 3,
        [
            (ANY, message_shape, F32),
            (VMEM, (rows, LANES), I32),
            (VMEM, (groups * (kmax + 8), LANES), I32),
            (SMEM, (blocks,), I32),
        ],
        [
            pltpu.VMEM((boxes, past_rows, LANES), F32),
            pltpu.SMEM((2 * boxes,), I32),
            pltpu.SemaphoreType.DMA,
        ],
    )(move_list, age_slot, past, tile_slot.T, tile_count.reshape(1, blocks))
    mates = [(box, box ^ 1) for box in range(boxes)]
    own_places, own_gammas, plan = lax.optimization_barrier((places, gammas, plan))
    mate_places = lax.ppermute(own_places, "box", mates)
    mate_gammas = lax.ppermute(own_gammas, "box", mates)
    labels, message, plan, ranked = lax.optimization_barrier((labels, message, plan, ranked))
    message = call(
        functools.partial(answer_kernel, blocks, boxes, rcap),
        "answer",
        [SMEM, VMEM, VMEM, ANY],
        (ANY, message_shape, F32),
        [pltpu.VMEM((boxes, 6 * rcap, LANES), F32), pltpu.SemaphoreType.DMA((4,))],
        {3: 0},
        limit=65400 << 10,
    )(labels, places, gammas, message)
    plan, ranked, message = lax.optimization_barrier((plan, ranked, message))
    fetched = swap(message)

    def scratch(owners):
        return [
            pltpu.VMEM((owners, 24 * 8, LANES), F32),
            pltpu.VMEM((owners, 64, LANES), F32),
            pltpu.VMEM((owners * rcap, LANES, LANES), BF),
            pltpu.VMEM((owners * rcap, 16, 2 * LANES), BF),
            pltpu.VMEM((blocks * 8, LANES), F32),
            pltpu.VMEM((blocks * 8, LANES), F32),
            pltpu.VMEM((UNROLL, 8, 2 * LANES), F32),
        ]

    partial, targets, centre, turns, moved_from, aged_from = call(
        functools.partial(near_kernel, blocks, boxes, rcap, cap, slots, kmax, most),
        "near",
        [SMEM] * 6 + [VMEM] * 5,
        [
            (VMEM, (blocks * 8, LANES), F32),
            (VMEM, (blocks, FEATURES, LANES), BF),
            (VMEM, (8, LANES), F32),
            (VMEM, (5, blocks, LANES), F32),
            (SMEM, (blocks,), I32),
            (SMEM, (blocks,), I32),
        ],
        [pltpu.VMEM((2 * 24 * 8, LANES), F32), pltpu.VMEM((2, 6 * rcap, LANES), F32)] + scratch(2),
    )(
        plan, ranked, asked, labels, hub_centre.T, azimuth,
        places, gammas, mate_places, mate_gammas, blade_id,
    )
    fetched, partial = lax.optimization_barrier((fetched, partial))
    new_positions, new_history, outgoing = call(
        functools.partial(far_kernel, blocks, boxes, rcap, cap, slots, kmax, most),
        "far",
        [SMEM] * 4 + [VMEM] * 5,
        [
            (VMEM, (3 * blocks, LANES), F32),
            (VMEM, (blocks, 3, 2, LANES), F32),
            (VMEM, (boxes, 3 * cap, LANES), F32),
        ],
        [pltpu.VMEM((3 * blocks, LANES), F32)] + scratch(boxes),
        limit=65400 << 10,
    )(plan, ranked, moved_from, age_place, fetched, places, targets, centre, partial)
    aged = swap(outgoing)
    frame = call(
        functools.partial(frame_kernel, blocks, cap),
        "frame",
        [SMEM, VMEM, VMEM],
        (VMEM, (3 * blocks, LANES), F32),
        limit=65400 << 10,
    )(aged_from, aged, turns)

    def back(rows):
        return jnp.transpose(rows.reshape(3, blocks, LANES), (1, 0, 2))

    return back(new_positions), jnp.transpose(new_history, (0, 2, 1, 3)), back(frame)


def solution(mesh):
    split = ("cases", "box")
    placed = (
        P(split, None, None),
        P(split, None, None),
        P(split, None, None, None),
        P(split),
        P(split),
        P(split, None, None),
        P(split, None),
        P(split),
        P(split, None),
        P("cases", None),
        P("cases"),
    )
    return jax.shard_map(
        body,
        mesh=mesh,
        in_specs=placed,
        out_specs=(P(split, None, None), P(split, None, None, None), P(split, None, None)),
        check_vma=False,
    )
```

```python
import functools
import math

import jax
import jax.numpy as jnp
from jax import lax
from jax.experimental import pallas as pl
from jax.experimental.pallas import tpu as pltpu
from jax.sharding import PartitionSpec as P

ROTORS = 6
BLADES = 3

core_square = 0.05
time_step = 0.05

LANES = 128
FEATURES = 32
UNROLL = 48
BUILD = 16
BF = jnp.bfloat16
F32 = jnp.float32
I32 = jnp.int32

SMEM = pl.BlockSpec(memory_space=pltpu.SMEM)
VMEM = pl.BlockSpec(memory_space=pltpu.VMEM)
ANY = pl.BlockSpec(memory_space=pl.ANY)


def split3(value):
    high = value.astype(BF).astype(F32)
    rest = value - high
    middle = rest.astype(BF).astype(F32)
    return high, middle, rest - middle


def iota(dims, axis):
    return lax.broadcasted_iota(I32, dims, axis)


def meta_kernel(blocks, boxes, rcap, cap, move, age, fetch, meta):
    def product(left, right, contract=1):
        return lax.dot_general(
            left.astype(BF), right.astype(BF), (((1,), (contract,)), ((), ())),
            preferred_element_type=F32,
        )

    def flag(condition):
        return jnp.where(condition, 1.0, 0.0)

    asked = product(flag(iota((boxes, boxes), 0) == iota((boxes, boxes), 1)), fetch[...].astype(F32), 1)
    row = product(asked, flag(iota((rcap, LANES), 0) == iota((rcap, LANES), 1)), 0)
    before = flag(iota((blocks, blocks), 0) < iota((blocks, blocks), 1))
    diagonal = iota((blocks, blocks), 0) == iota((blocks, blocks), 1)
    lane = iota((blocks, LANES), 1)
    for n, source in enumerate((move, age)):
        block = source[...]
        sent = flag(lax.div(block, blocks) == iota((boxes, blocks), 0))
        rank = jnp.sum(sent * product(sent, before, 0), axis=0, keepdims=True)
        turned = product(jnp.where(diagonal, rank, 0.0), jnp.ones((blocks, LANES), F32), 0)
        place = flag(turned.astype(I32) + (rcap + n * cap) == lane)
        row = row + product(sent * lax.rem(block, blocks).astype(F32), place, 0)
        row = row + product(sent, flag(lane == rcap + 2 * cap + n), 0)
    meta[...] = row.astype(I32)


def plan_rows(slots, most):
    chunks = (most + LANES - 1) // LANES
    users = (slots + BUILD + LANES - 1) // LANES
    return chunks, users, (2 * chunks + users + 3 + 7) // 8 * 8


def plan_kernel(blocks, boxes, kmax, rcap, cap, slots, most, move, age, history, tiles, count,
                message, plan, ranked, age_place, packed, filled, sem):
    def clear(p, carry):
        filled[p] = 0
        return carry

    lax.fori_loop(0, 2 * boxes, clear, 0, unroll=8)
    shift = blocks.bit_length() - 1

    def owner(block):
        return block >> shift if 1 << shift == blocks else lax.div(block, blocks)

    def one(g, carry):
        box = owner(age[g])
        rank = filled[boxes + box]
        filled[boxes + box] = rank + 1
        age_place[g] = box * 256 + rank
        box = owner(move[g])
        rank = filled[box]
        filled[box] = rank + 1
        for axis in range(3):
            packed[box, pl.ds(axis * cap + rank, 2, stride=3 * cap), :] = history[g, axis]
        return carry

    lax.fori_loop(0, blocks, one, 0, unroll=8)
    sent = pltpu.make_async_copy(packed, message.at[:, pl.ds(6 * rcap, packed.shape[1]), :], sem)
    sent.start()
    half = kmax
    near = 2 * rcap
    chunks, users, rows = plan_rows(slots, most)
    turn = lax.axis_index("box") * rcap
    slot = iota((slots, blocks), 0) ^ turn
    times = jnp.zeros((slots, blocks), I32)
    for k in range(kmax):
        named = jnp.where(count[...] > k, tiles[k : k + 1, :], -1)
        times = times + jnp.where(slot == named, 1, 0)
    present = jnp.where(times > 0, 1.0, 0.0)
    inner = jnp.where(iota((blocks, blocks), 0) < iota((blocks, blocks), 1), 1.0, 0.0)
    rank = jnp.dot(present.astype(BF), inner.astype(BF), preferred_element_type=F32)
    rank = jnp.where(times > 0, rank, -2.0)
    number = jnp.dot(
        present.astype(BF), jnp.ones((blocks, LANES), BF), preferred_element_type=F32
    ).astype(I32)
    pairs = (number + 1) >> 1
    outer = jnp.where(iota((slots, slots), 1) <= iota((slots, slots), 0), 1.0, 0.0).astype(BF)
    ends = jnp.dot(outer, pairs.astype(F32).astype(BF), preferred_element_type=F32).astype(I32)
    used = jnp.where(number > 0, 1.0, 0.0).astype(BF)
    tally = jnp.dot(outer, used, preferred_element_type=F32).astype(I32)
    lane = iota((1, LANES), 1)

    def first_after(done):
        return jnp.sum(jnp.where(tally <= done, 1, 0), axis=0, keepdims=True)

    begin = jnp.zeros((1, LANES), I32)
    behind = jnp.zeros((1, LANES), I32)
    for part, last in ((0, near), (1, slots)):
        stop = ends[last - 1 : last, :]
        opening = first_after(behind)
        for chunk in range(chunks):
            spot = begin + lane + chunk * LANES
            past = ends <= spot
            source = jnp.sum(jnp.where(past, 1, 0), axis=0, keepdims=True)
            start = jnp.max(jnp.where(past, ends, 0), axis=0, keepdims=True)
            word = jnp.where(spot < stop, source + (spot - start) * 65536, opening + half * 65536)
            row = part * chunks + chunk
            plan[row : row + 1, :] = word
        row = rows - 3 + part
        plan[row : row + 1, :] = lax.div(stop - begin + (UNROLL - 1), UNROLL)
        if part == 0:
            begin = stop
            behind = tally[last - 1 : last, :]
    live = tally[slots - 1 : slots, :]
    for chunk in range(users):
        spot = behind + lane + chunk * LANES
        row = 2 * chunks + chunk
        plan[row : row + 1, :] = jnp.where(spot < live, first_after(spot), first_after(behind))
    plan[rows - 1 : rows, :] = (live - behind + (BUILD - 1)) >> (BUILD.bit_length() - 1)
    limit = jnp.max(pairs)
    for group in range(slots // LANES):
        at = slice(group * LANES, (group + 1) * LANES)
        wide = [
            jnp.concatenate([value, jnp.zeros((LANES, LANES - blocks), F32)], axis=1).T[:blocks]
            for value in (rank[at], times[at].astype(F32))
        ]
        position = wide[0].astype(I32)
        entry = iota((blocks, LANES), 0) + wide[1].astype(I32) * 256
        entry = jnp.where((position & 1) == 1, entry * 65536, entry)
        position = position >> 1
        first = group * (half + 8)
        ranked[first + half : first + half + 8, :] = jnp.zeros((8, LANES), I32)

        def fill(t, carry):
            found = jnp.sum(jnp.where(position == t, entry, 0), axis=0, keepdims=True)
            ranked[pl.ds(first + t, 1), :] = found
            return carry

        lax.fori_loop(0, limit, fill, 0)
    sent.wait()


def target_features(blocks, positions, blade, hub, azimuth, feats, centre, tables, stage):
    middle = [
        jnp.sum(positions[axis * blocks : (axis + 1) * blocks, :], axis=(0, 1), keepdims=True)
        / (blocks * LANES)
        for axis in range(3)
    ]
    for axis in range(3):
        centre[axis : axis + 1, :] = jnp.broadcast_to(middle[axis], (1, LANES))
    ones = jnp.ones((8, LANES), F32)
    pad = jnp.zeros((FEATURES - 24, LANES), F32)
    for group in range(blocks // 8):
        first = group * 8
        at = [
            positions[axis * blocks + first : axis * blocks + first + 8, :] - middle[axis]
            for axis in range(3)
        ]
        norm = split3(at[0] * at[0] + at[1] * at[1] + at[2] * at[2] + core_square)
        parts = [split3(-2.0 * value) for value in at]
        rows = []
        for piece in (0, 1, 2, 0, 1, 0):
            rows += [parts[axis][piece] for axis in range(3)]
        rows += [ones, ones, ones, norm[0], norm[1], norm[2]]
        base = (group % 2) * 24 * 8
        for f, value in enumerate(rows):
            stage[base + f * 8 : base + f * 8 + 8, :] = value
        for t in range(8):
            picked = stage[pl.ds(base + t, 24, stride=8), :]
            feats[first + t] = jnp.concatenate([picked, pad], axis=0).astype(BF)
    lane = iota((8, LANES), 1)
    angle = jnp.zeros((8, LANES), F32)
    hubs = [jnp.zeros((8, LANES), F32) for _ in range(3)]
    for q in range(ROTORS * BLADES):
        turn = F32(2.0 * math.pi) * F32(q % BLADES) / F32(BLADES)
        angle = jnp.where(lane == q, azimuth[q // BLADES] + turn, angle)
        for axis in range(3):
            hubs[axis] = jnp.where(lane == q, hub[axis, q // BLADES], hubs[axis])
    sources = [jnp.cos(angle), jnp.sin(angle)] + hubs
    for group in range(blocks // 8):
        index = blade[group * 8 : group * 8 + 8, :]
        for n, source in enumerate(sources):
            tables[n, group * 8 : group * 8 + 8, :] = jnp.take_along_axis(source, index, axis=1)


def answer_kernel(blocks, boxes, rcap, asked, positions, strengths, _, message, packed, sems):
    quarter = boxes // 4
    sent = []
    for part in range(4):
        first = part * quarter

        def one(p, carry):
            for i in range(rcap):
                block = jnp.maximum(asked[p, i], 0)
                packed[p, pl.ds(i, 3, stride=rcap), :] = positions[pl.ds(block, 3, stride=blocks), :]
                packed[p, pl.ds(3 * rcap + i, 3, stride=rcap), :] = strengths[
                    pl.ds(block, 3, stride=blocks), :
                ]
            return carry

        lax.fori_loop(first, first + quarter, one, 0, unroll=4)
        peers = pl.ds(first, quarter)
        copy = pltpu.make_async_copy(
            packed.at[peers], message.at[peers, pl.ds(0, 6 * rcap), :], sems.at[part]
        )
        copy.start()
        sent.append(copy)
    for copy in sent:
        copy.wait()


def prepare(source, centre, rcap, stage, table_stage, o):
    ones = jnp.ones((8, LANES), F32)
    zeros = jnp.zeros((8, LANES), F32)
    at = [source(axis) - centre[axis : axis + 1, :] for axis in range(3)]
    gamma = [source(3 + axis) for axis in range(3)]
    parts = [split3(value) for value in at]
    norm = split3(at[0] * at[0] + at[1] * at[1] + at[2] * at[2])
    values = []
    for piece in (0, 0, 0, 1, 1, 2):
        values += [parts[axis][piece] for axis in range(3)]
    values += [norm[0], norm[1], norm[2], ones, ones, ones]
    for f, value in enumerate(values):
        stage[o, f * 8 : f * 8 + 8, :] = value
    for axis in range(3):
        left, right = (axis + 1) % 3, (axis + 2) % 3
        table_stage[o, axis * 8 : axis * 8 + 8, :] = gamma[axis]
        table_stage[o, (3 + axis) * 8 : (4 + axis) * 8, :] = (
            at[left] * gamma[right] - at[right] * gamma[left]
        )
    table_stage[o, 48:56, :] = zeros
    table_stage[o, 56:64, :] = zeros


def build(slot, identity, stage, table_stage, feats, tables):
    zeros = jnp.zeros((8, LANES), F32)
    pad = jnp.zeros((LANES - 24, LANES), F32)
    o = slot >> 3
    i = slot & 7
    picked = jnp.concatenate([stage[o, pl.ds(i, 24, stride=8), :], pad], axis=0)
    turned = lax.dot_general(
        identity, picked.astype(BF), (((1,), (1,)), ((), ())), preferred_element_type=F32
    )
    feats[slot] = turned.astype(BF)
    table = table_stage[o, pl.ds(i, 8, stride=8), :]
    high = table.astype(BF).astype(F32)
    left = jnp.concatenate([high, table - high], axis=0)
    right = jnp.concatenate([high, zeros], axis=0)
    tables[slot] = jnp.concatenate([left, right], axis=1).astype(BF)


def unit():
    return jnp.where(iota((LANES, LANES), 0) == iota((LANES, LANES), 1), 1.0, 0.0).astype(BF)


def gather_pairs(first, number, slots, half, plan, ranked, targets, feats, tables, sums0, sums1, held):
    held[...] = jnp.zeros_like(held)
    empty = jnp.zeros((LANES - FEATURES, 2 * LANES), BF)

    def named(it):
        found = []
        for u in range(UNROLL):
            at = it * UNROLL + u
            word = plan[first + (at >> 7), at & 127]
            slot = word & 65535
            row = word >> 16
            if slots > LANES:
                row = row + (slot >> 7) * (half + 8)
            found.append((slot, ranked[row, slot & 127]))
        return found

    def flush(it):
        for u, (_, pair) in enumerate(named(it)):
            for sums, word, part in (
                (sums0, pair & 65535, held[u, :, :LANES]),
                (sums1, pair >> 16, held[u, :, LANES:]),
            ):
                at = pl.ds(pl.multiple_of((word & 255) * 8, 8), 8)
                sums[at, :] = sums[at, :] + (word >> 8).astype(F32) * part

    def accumulate(it, carry):
        flush(jnp.maximum(it - 1, 0))
        for u, (slot, pair) in enumerate(named(it)):
            both = jnp.concatenate([targets[pair & 255], targets[(pair >> 16) & 255]], axis=1)
            both = jnp.concatenate([both, empty], axis=0)
            inverse = lax.rsqrt(jnp.dot(feats[slot], both, preferred_element_type=F32))
            weight = inverse * inverse * inverse
            high = weight.astype(BF)
            low = (weight - high.astype(F32)).astype(BF)
            summed = jnp.dot(
                tables[slot], jnp.concatenate([high, low], axis=0), preferred_element_type=F32
            )
            held[u] = summed[:8] + summed[8:]
        return carry

    lax.fori_loop(0, number, accumulate, 0)

    @pl.when(number > 0)
    def _():
        flush(number - 1)


def near_kernel(blocks, boxes, rcap, cap, slots, half, most, plan, ranked, asked, labels, hub,
                azimuth, places, gammas, mate_places, mate_gammas, blade,
                partial, targets, centre, turns, moved_from, aged_from,
                target_stage, local, stage, table_stage, feats, tables, sums0, sums1, held):
    target_features(blocks, places, blade, hub, azimuth, targets, centre, turns, target_stage)

    def peer(p, carry):
        for target, lane, number in ((moved_from, rcap, 0), (aged_from, rcap + cap, 1)):

            def label(rank, carry):
                target[labels[p, lane + rank]] = p * 256 + rank
                return carry

            lax.fori_loop(0, labels[p, rcap + 2 * cap + number], label, 0)
        return carry

    lax.fori_loop(0, boxes, peer, 0)
    _, _, rows = plan_rows(slots, most)
    me = lax.axis_index("box")
    for o, (from_places, from_gammas) in enumerate(((places, gammas), (mate_places, mate_gammas))):
        for i in range(rcap):
            block = jnp.maximum(asked[i, me ^ o], 0)
            local[o, pl.ds(i, 3, stride=rcap), :] = from_places[pl.ds(block, 3, stride=blocks), :]
            local[o, pl.ds(3 * rcap + i, 3, stride=rcap), :] = from_gammas[
                pl.ds(block, 3, stride=blocks), :
            ]
    for o in range(2):
        prepare(
            lambda c: local[o, c * rcap : (c + 1) * rcap, :], centre, rcap, stage, table_stage, o
        )
    identity = unit()
    for slot in range(2 * rcap):
        build(slot, identity, stage, table_stage, feats, tables)
    sums0[...] = jnp.zeros_like(sums0)
    sums1[...] = jnp.zeros_like(sums1)
    gather_pairs(
        0, plan[rows - 3, 0], slots, half, plan, ranked, targets, feats, tables, sums0, sums1, held
    )
    partial[...] = sums0[...] + sums1[...]


def far_kernel(blocks, boxes, rcap, cap, slots, half, most, plan, ranked, moved_from, age_place,
               fetched, positions, targets, centre, partial,
               new_positions, new_history, outgoing,
               speed, stage, table_stage, feats, tables, sums0, sums1, held):
    chunks, _, rows = plan_rows(slots, most)
    me = lax.axis_index("box")

    def owner(o, carry):
        at = o ^ me
        prepare(
            lambda c: fetched[at, c * rcap : (c + 1) * rcap, :], centre, rcap, stage, table_stage, o
        )
        return carry

    lax.fori_loop(2, boxes, owner, 0, unroll=2)
    identity = unit()

    def several(it, carry):
        for u in range(BUILD):
            at = it * BUILD + u
            slot = plan[2 * chunks + (at >> 7), at & 127]
            build(slot, identity, stage, table_stage, feats, tables)
        return carry

    lax.fori_loop(0, plan[rows - 1, 0], several, 0)
    sums0[...] = partial[...]
    sums1[...] = jnp.zeros_like(sums1)
    gather_pairs(
        chunks, plan[rows - 2, 0], slots, half, plan, ranked, targets, feats, tables,
        sums0, sums1, held,
    )
    scale = 1.0 / (4.0 * math.pi)
    for group in range(blocks // 8):
        first = group * 8
        total = [
            sums0[pl.ds(first * 8 + f, 8, stride=8), :] + sums1[pl.ds(first * 8 + f, 8, stride=8), :]
            for f in range(6)
        ]
        at = [
            positions[axis * blocks + first : axis * blocks + first + 8, :]
            - centre[axis : axis + 1, :]
            for axis in range(3)
        ]
        for axis in range(3):
            left, right = (axis + 1) % 3, (axis + 2) % 3
            speed[axis * blocks + first : axis * blocks + first + 8, :] = scale * (
                at[left] * total[right] - at[right] * total[left] - total[3 + axis]
            )
    unused = jnp.zeros((3 * cap, LANES), F32)

    def clear(p, carry):
        outgoing[p] = unused
        return carry

    lax.fori_loop(0, boxes, clear, 0)

    def finish(b, carry):
        where = moved_from[b]
        box = where >> 8
        rank = where & 255
        recent = fetched[box, pl.ds(6 * rcap + rank, 3, stride=cap), :]
        older = fetched[box, pl.ds(6 * rcap + 3 * cap + rank, 3, stride=cap), :]
        rows = pl.ds(b, 3, stride=blocks)
        now = speed[rows, :]
        stepped = positions[rows, :] + time_step * (23.0 * now - 16.0 * recent + 5.0 * older) / 12.0
        new_positions[rows, :] = stepped
        for axis in range(3):
            new_history[b, axis, 0:1, :] = now[axis : axis + 1]
            new_history[b, axis, 1:2, :] = recent[axis : axis + 1]
        out = age_place[b]
        outgoing[out >> 8, pl.ds(out & 255, 3, stride=cap), :] = stepped
        return carry

    lax.fori_loop(0, blocks, finish, 0, unroll=4)


def frame_kernel(blocks, cap, aged_from, arrived, tables, frame):
    def one(b, carry):
        where = aged_from[b]
        aged = arrived[where >> 8, pl.ds(where & 255, 3, stride=cap), :]
        cosine, sine, hub0, hub1, hub2 = [tables[n, pl.ds(b, 1), :] for n in range(5)]
        first = aged[0:1] - hub0
        second = aged[1:2] - hub1
        frame[pl.ds(b, 1), :] = cosine * first + sine * second
        frame[pl.ds(blocks + b, 1), :] = cosine * second - sine * first
        frame[pl.ds(2 * blocks + b, 1), :] = aged[2:3] - hub2
        return carry

    lax.fori_loop(0, blocks, one, 0, unroll=8)


def swap(values):
    return lax.all_to_all(values, "box", split_axis=0, concat_axis=0, tiled=True)


def call(kernel, name, in_specs, outs, scratch=(), aliases={}, limit=64 << 20):
    several = isinstance(outs, list)
    listed = outs if several else [outs]
    specs = [spec for spec, _, _ in listed]
    shapes = [jax.ShapeDtypeStruct(dims, dtype) for _, dims, dtype in listed]
    return pl.pallas_call(
        kernel,
        in_specs=in_specs,
        out_specs=specs if several else specs[0],
        out_shape=shapes if several else shapes[0],
        scratch_shapes=list(scratch),
        input_output_aliases=aliases,
        compiler_params=pltpu.CompilerParams(vmem_limit_bytes=limit),
        name=name,
    )


def body(
    positions,
    strengths,
    history,
    move_list,
    age_slot,
    fetch_list,
    tile_slot,
    tile_count,
    blade_id,
    hub_centre,
    azimuth,
):
    blocks = positions.shape[0]
    boxes = lax.axis_size("box")
    rcap = fetch_list.shape[2]
    kmax = tile_slot.shape[1]
    cap = 2 * blocks // boxes
    slots = boxes * rcap
    most = (blocks * kmax + slots) // 2 + UNROLL
    chunks, users, rows = plan_rows(slots, most)
    groups = slots // LANES

    places = jnp.transpose(positions, (1, 0, 2)).reshape(3 * blocks, LANES)
    gammas = jnp.transpose(strengths, (1, 0, 2)).reshape(3 * blocks, LANES)
    past = jnp.transpose(history, (0, 2, 1, 3))

    asked = fetch_list[0].T
    meta = call(
        functools.partial(meta_kernel, blocks, boxes, rcap, cap),
        "meta",
        [VMEM] * 3,
        (VMEM, (boxes, LANES), I32),
    )(move_list.reshape(1, blocks), age_slot.reshape(1, blocks), asked)
    labels = swap(meta)
    past_rows = (6 * cap + 7) // 8 * 8
    message_shape = (boxes, 6 * rcap + past_rows, LANES)
    message, plan, ranked, age_place = call(
        functools.partial(plan_kernel, blocks, boxes, kmax, rcap, cap, slots, most),
        "plan",
        [SMEM] * 2 + [VMEM] * 3,
        [
            (ANY, message_shape, F32),
            (VMEM, (rows, LANES), I32),
            (VMEM, (groups * (kmax + 8), LANES), I32),
            (SMEM, (blocks,), I32),
        ],
        [
            pltpu.VMEM((boxes, past_rows, LANES), F32),
            pltpu.SMEM((2 * boxes,), I32),
            pltpu.SemaphoreType.DMA,
        ],
    )(move_list, age_slot, past, tile_slot.T, tile_count.reshape(1, blocks))
    mates = [(box, box ^ 1) for box in range(boxes)]
    own_places, own_gammas, plan = lax.optimization_barrier((places, gammas, plan))
    mate_places = lax.ppermute(own_places, "box", mates)
    mate_gammas = lax.ppermute(own_gammas, "box", mates)
    labels, message, plan, ranked = lax.optimization_barrier((labels, message, plan, ranked))
    message = call(
        functools.partial(answer_kernel, blocks, boxes, rcap),
        "answer",
        [SMEM, VMEM, VMEM, ANY],
        (ANY, message_shape, F32),
        [pltpu.VMEM((boxes, 6 * rcap, LANES), F32), pltpu.SemaphoreType.DMA((4,))],
        {3: 0},
        limit=65400 << 10,
    )(labels, places, gammas, message)
    plan, ranked, message = lax.optimization_barrier((plan, ranked, message))
    fetched = swap(message)

    def scratch(owners):
        return [
            pltpu.VMEM((owners, 24 * 8, LANES), F32),
            pltpu.VMEM((owners, 64, LANES), F32),
            pltpu.VMEM((owners * rcap, LANES, LANES), BF),
            pltpu.VMEM((owners * rcap, 16, 2 * LANES), BF),
            pltpu.VMEM((blocks * 8, LANES), F32),
            pltpu.VMEM((blocks * 8, LANES), F32),
            pltpu.VMEM((UNROLL, 8, 2 * LANES), F32),
        ]

    partial, targets, centre, turns, moved_from, aged_from = call(
        functools.partial(near_kernel, blocks, boxes, rcap, cap, slots, kmax, most),
        "near",
        [SMEM] * 6 + [VMEM] * 5,
        [
            (VMEM, (blocks * 8, LANES), F32),
            (VMEM, (blocks, FEATURES, LANES), BF),
            (VMEM, (8, LANES), F32),
            (VMEM, (5, blocks, LANES), F32),
            (SMEM, (blocks,), I32),
            (SMEM, (blocks,), I32),
        ],
        [pltpu.VMEM((2 * 24 * 8, LANES), F32), pltpu.VMEM((2, 6 * rcap, LANES), F32)] + scratch(2),
    )(
        plan, ranked, asked, labels, hub_centre.T, azimuth,
        places, gammas, mate_places, mate_gammas, blade_id,
    )
    fetched, partial = lax.optimization_barrier((fetched, partial))
    new_positions, new_history, outgoing = call(
        functools.partial(far_kernel, blocks, boxes, rcap, cap, slots, kmax, most),
        "far",
        [SMEM] * 4 + [VMEM] * 5,
        [
            (VMEM, (3 * blocks, LANES), F32),
            (VMEM, (blocks, 3, 2, LANES), F32),
            (VMEM, (boxes, 3 * cap, LANES), F32),
        ],
        [pltpu.VMEM((3 * blocks, LANES), F32)] + scratch(boxes),
        limit=65400 << 10,
    )(plan, ranked, moved_from, age_place, fetched, places, targets, centre, partial)
    aged = swap(outgoing)
    frame = call(
        functools.partial(frame_kernel, blocks, cap),
        "frame",
        [SMEM, VMEM, VMEM],
        (VMEM, (3 * blocks, LANES), F32),
        limit=65400 << 10,
    )(aged_from, aged, turns)

    def back(rows):
        return jnp.transpose(rows.reshape(3, blocks, LANES), (1, 0, 2))

    return back(new_positions), jnp.transpose(new_history, (0, 2, 1, 3)), back(frame)


def solution(mesh):
    split = ("cases", "box")
    placed = (
        P(split, None, None),
        P(split, None, None),
        P(split, None, None, None),
        P(split),
        P(split),
        P(split, None, None),
        P(split, None),
        P(split),
        P(split, None),
        P("cases", None),
        P("cases"),
    )
    return jax.shard_map(
        body,
        mesh=mesh,
        in_specs=placed,
        out_specs=(P(split, None, None), P(split, None, None, None), P(split, None, None)),
        check_vma=False,
    )
```
